256 devices in a mesh: wide: 64 (over z_lo, x, y), narrow: 4 (over z_hi, core).
Axes of the slice: x: 4, y: 4, z: 8 (z_hi: 2, z_lo: 4; z = z_hi * 4 + z_lo), core: 2. Of those that a mesh axis runs over, the one named last changes fastest.
Arguments:
- constraint_mats: bfloat16 [1024, 256, 256], P(('narrow', 'wide')), may hold values from -0.375 to 0.375
- primal_matrix: bfloat16 [256, 256], replicated, may hold values from -0.25 to 0.25
- inverse_dual_iterate: bfloat16 [256, 256], replicated, may hold values from -0.25 to 0.25
Outputs:
- schur: float32 [1024, 1024], P(('narrow', 'wide'))
The draws below stay inside these ranges and needn't reach their ends.
All inputs are finite; a program needn't handle non-finite values.
Results may differ from the reference program's by a relative error of at most 0.0029.
Values may be sent and summed in bfloat16 or wider, within the bound.
A program may use at most 64 MiB of HBM per device.

```python
import jax
import jax.numpy as jnp

ORDER = 256
M_TOT = 1024


def symmetric_draw(key, shape, scale, limit):
    raw = jnp.clip(jax.random.normal(key, shape, jnp.float32) * scale, -limit, limit)
    return 0.5 * (raw + jnp.swapaxes(raw, -1, -2))


def draw_constraint_mats(key, part):
    return symmetric_draw(key, (M_TOT, ORDER, ORDER), 0.0625, 0.375).astype(jnp.bfloat16)


def draw_primal_matrix(key, part):
    return symmetric_draw(jax.random.fold_in(key, 11), (ORDER, ORDER), 0.0625, 0.25).astype(jnp.bfloat16)


def draw_inverse_dual_iterate(key, part):
    return symmetric_draw(jax.random.fold_in(key, 23), (ORDER, ORDER), 0.0625, 0.25).astype(jnp.bfloat16)


def setup_inputs(seed: int = 0) -> dict:
    keys = jax.random.split(jax.random.key(seed), 4)
    constraint_mats = draw_constraint_mats(jax.random.fold_in(keys[3], 71), 0)
    primal_matrix = draw_primal_matrix(jax.random.fold_in(keys[3], 71), 0)
    inverse_dual_iterate = draw_inverse_dual_iterate(jax.random.fold_in(keys[3], 71), 0)
    return {"constraint_mats": constraint_mats, "primal_matrix": primal_matrix, "inverse_dual_iterate": inverse_dual_iterate}


def reference(constraint_mats, primal_matrix, inverse_dual_iterate):
    mats = constraint_mats.astype(jnp.float32)
    left_product = jnp.einsum('ab,ibc->iac', primal_matrix.astype(jnp.float32), mats).astype(jnp.bfloat16)
    product_matrices = jnp.einsum('lsx,xm->lsm', left_product.astype(jnp.float32), inverse_dual_iterate.astype(jnp.float32)).astype(jnp.bfloat16)
    count = constraint_mats.shape[0]
    u_flat = product_matrices.reshape(count, -1).astype(jnp.float32)
    a_flat = mats.reshape(count, -1)
    pairing = jnp.dot(u_flat, a_flat.T)
    return 0.5 * (pairing + pairing.T)
```

```python
import jax
import jax.numpy as jnp
from jax import lax
from jax.experimental import pallas as pl
from jax.experimental.pallas import tpu as pltpu
from jax.sharding import PartitionSpec as P

PARTS = 16
LINE = 4
COUNT = 4
ROWS = 16
LANES = 128
SLICE = 2 * COUNT * ROWS + 2 * COUNT
DEPTH = (ROWS + 1) * LANES
GROUP = PARTS * COUNT


def dot(a, b):
    return lax.dot_general(a, b, (((1,), (0,)), ((), ())), preferred_element_type=jnp.float32)


def dot_nt(a, b):
    return lax.dot_general(a, b, (((1,), (1,)), ((), ())), preferred_element_type=jnp.float32)


def kernel(a_ref, x_ref, z_ref, out_ref, send1, recv1, wide_rows, diag_rows, v_all, a_own, a_all, partial, send3, recv3,
           send4, recv4, joined, s1, r1, s2v, r2v, s2a, r2a, s3, r3, s4, r4, own_sem):
    wide, narrow = lax.axis_index("wide"), lax.axis_index("narrow")
    y = lax.rem(wide, 4)
    x = lax.rem(lax.div(wide, 4), 4)
    z_lo = lax.div(wide, 16)
    part = narrow * 4 + z_lo

    def in_column(p):
        return {"wide": lax.rem(p, 4) * 16 + x * 4 + y, "narrow": lax.div(p, 4)}

    def along_x(k):
        return {"wide": z_lo * 16 + k * 4 + y, "narrow": narrow}

    def along_y(k):
        return {"wide": z_lo * 16 + x * 4 + k, "narrow": narrow}

    barrier = pltpu.get_barrier_semaphore()
    for k in range(1, PARTS):
        pl.semaphore_signal(barrier, inc=1, device_id=in_column(lax.rem(part + k, PARTS)))
    for k in range(1, LINE):
        pl.semaphore_signal(barrier, inc=1, device_id=along_x(lax.rem(x + k, LINE)))
        pl.semaphore_signal(barrier, inc=1, device_id=along_y(lax.rem(y + k, LINE)))

    row = lax.broadcasted_iota(jnp.int32, (LANES, LANES), 0)
    col = lax.broadcasted_iota(jnp.int32, (LANES, LANES), 1)
    primal, dual = x_ref[...], z_ref[...]
    diag_a, diag_v = [], []
    for c in range(COUNT):
        mat = a_ref[c]
        left = dot(primal, mat).astype(jnp.bfloat16)
        top = dot(left[:LANES], dual) + dot_nt(dual[:LANES], left)
        low = dot(left[LANES:], dual[:, LANES:]) + dot_nt(dual[LANES:], left[LANES:])
        mat32 = mat.astype(jnp.float32)
        a_up, a_low = mat32[:LANES, :LANES], mat32[LANES:, LANES:]
        fold_a = [mat[:LANES, LANES:], jnp.where(row <= col, a_up, a_low).astype(jnp.bfloat16)]
        corner = jnp.where(row < col, top[:, :LANES], jnp.where(row == col, 0.5 * top[:, :LANES], low))
        fold_v = [top[:, LANES:].astype(jnp.bfloat16), corner.astype(jnp.bfloat16)]
        diag_a.append(jnp.sum(jnp.where(row == col, a_low, 0.0), axis=0, keepdims=True))
        diag_v.append(jnp.sum(jnp.where(row == col, low, 0.0), axis=0, keepdims=True) * (0.5 / PARTS))
        for d in range(PARTS):
            half, at = d // 8, (d % 8) * ROWS
            send1[d, ROWS * c:ROWS * (c + 1), :] = fold_a[half][at:at + ROWS]
            send1[d, ROWS * (COUNT + c):ROWS * (COUNT + c + 1), :] = fold_v[half][at:at + ROWS]
    diag = jnp.concatenate(diag_a + diag_v, axis=0).astype(jnp.bfloat16)
    for d in range(PARTS):
        send1[d, 2 * COUNT * ROWS:, :] = diag

    pl.semaphore_wait(barrier, PARTS - 1 + 2 * (LINE - 1))

    def copy1(slot, to):
        return pltpu.make_async_remote_copy(
            src_ref=send1.at[to], dst_ref=recv1.at[slot], send_sem=s1.at[to], recv_sem=r1.at[slot], device_id=in_column(to)
        )

    for k in range(1, PARTS):
        copy1(part, lax.rem(part + k, PARTS)).start()
    own = pltpu.make_async_copy(send1.at[part], recv1.at[part], own_sem)
    own.start()
    own.wait()
    for k in range(1, PARTS):
        src = lax.rem(part + k, PARTS)
        copy1(src, src).wait_recv()

    for s in range(PARTS):
        block = recv1[s].astype(jnp.float32)
        wide_rows[0, GROUP * s:GROUP * (s + 1), :] = block[:GROUP]
        wide_rows[1, GROUP * s:GROUP * (s + 1), :] = block[GROUP:2 * GROUP]
        diag_rows[0, COUNT * s:COUNT * (s + 1), :] = block[2 * GROUP:2 * GROUP + COUNT]
        diag_rows[1, COUNT * s:COUNT * (s + 1), :] = block[2 * GROUP + COUNT:]
    for r in range(ROWS):
        at = pl.ds(r * LANES, LANES)
        part_a = wide_rows[0, pl.ds(r, GROUP, stride=ROWS), :].astype(jnp.bfloat16)
        for n in range(LINE):
            a_own[n, :, at] = part_a[ROWS * n:ROWS * (n + 1)]
        v_all[y, :, at] = wide_rows[1, pl.ds(r, GROUP, stride=ROWS), :].astype(jnp.bfloat16)
    at = pl.ds(ROWS * LANES, LANES)
    part_a = diag_rows[0].astype(jnp.bfloat16)
    for n in range(LINE):
        a_own[n, :, at] = part_a[ROWS * n:ROWS * (n + 1)]
    v_all[y, :, at] = diag_rows[1].astype(jnp.bfloat16)

    def copy_v(slot, to):
        return pltpu.make_async_remote_copy(
            src_ref=v_all.at[slot], dst_ref=v_all.at[slot], send_sem=s2v.at[to], recv_sem=r2v.at[slot], device_id=along_y(to)
        )

    def copy_a(slot, to):
        return pltpu.make_async_remote_copy(
            src_ref=a_own, dst_ref=a_all.at[:, slot], send_sem=s2a.at[to], recv_sem=r2a.at[slot], device_id=along_x(to)
        )

    for k in (2, 1, 3):
        copy_v(y, lax.rem(y + k, LINE)).start()
        copy_a(x, lax.rem(x + k, LINE)).start()
    own = pltpu.make_async_copy(a_own, a_all.at[:, x], own_sem)
    own.start()
    own.wait()
    for k in (1, 3, 2):
        src = lax.rem(y + k, LINE)
        copy_v(src, src).wait_recv()
        src = lax.rem(x + k, LINE)
        copy_a(src, src).wait_recv()

    partial[...] = dot_nt(
        v_all[...].reshape(LINE * GROUP, DEPTH), a_all[...].reshape(LINE * GROUP, DEPTH)
    )
    for p in range(PARTS):
        for k in range(LINE):
            send3[p, COUNT * k:COUNT * (k + 1), :] = partial[GROUP * k + COUNT * p:GROUP * k + COUNT * (p + 1), :]

    def copy3(slot, to):
        return pltpu.make_async_remote_copy(
            src_ref=send3.at[to], dst_ref=recv3.at[slot], send_sem=s3.at[to], recv_sem=r3.at[slot], device_id=in_column(to)
        )

    for k in range(1, PARTS):
        copy3(part, lax.rem(part + k, PARTS)).start()
    total = send3[part]
    for k in range(1, PARTS):
        src = lax.rem(part + k, PARTS)
        copy3(src, src).wait_recv()
        total = total + recv3[src]
    for k in range(LINE):
        send4[k] = total[COUNT * k:COUNT * (k + 1)]

    def copy4(slot, to):
        return pltpu.make_async_remote_copy(
            src_ref=send4.at[to], dst_ref=recv4.at[slot], send_sem=s4.at[to], recv_sem=r4.at[slot], device_id=along_y(to)
        )

    for k in range(1, LINE):
        copy4(y, lax.rem(y + k, LINE)).start()
    recv4[y] = send4[y]
    for k in range(1, LINE):
        src = lax.rem(y + k, LINE)
        copy4(src, src).wait_recv()

    for k in range(LINE):
        piece = recv4[k]
        for n in range(LINE):
            joined[COUNT * n:COUNT * (n + 1), GROUP * k:GROUP * (k + 1)] = piece[:, GROUP * n:GROUP * (n + 1)]
    wide_row = lax.broadcasted_iota(jnp.int32, (4 * GROUP, 4 * GROUP), 0)
    wide_col = lax.broadcasted_iota(jnp.int32, (4 * GROUP, 4 * GROUP), 1)
    digit = lambda v, size: lax.rem(lax.div(v, size), 4)
    source = digit(wide_col, 4) * 64 + digit(wide_col, 16) * 16 + digit(wide_col, 64) * 4 + digit(wide_col, 1)
    pick = jnp.where(wide_row == source, 1.0, 0.0).astype(jnp.bfloat16)
    value = joined[...]
    high = value.astype(jnp.bfloat16)
    rest = value - high.astype(jnp.float32)
    mid = rest.astype(jnp.bfloat16)
    low = (rest - mid.astype(jnp.float32)).astype(jnp.bfloat16)
    ordered = dot(high, pick) + dot(mid, pick) + dot(low, pick)
    for n in range(LINE):
        out_ref[:, 4 * GROUP * n:4 * GROUP * (n + 1)] = ordered[COUNT * n:COUNT * (n + 1)]

    for k in range(1, PARTS):
        to = lax.rem(part + k, PARTS)
        copy1(part, to).wait_send()
        copy3(part, to).wait_send()
    for k in range(1, LINE):
        to = lax.rem(y + k, LINE)
        copy_v(y, to).wait_send()
        copy4(y, to).wait_send()
        copy_a(x, lax.rem(x + k, LINE)).wait_send()


def body(constraint_mats, primal_matrix, inverse_dual_iterate):
    vmem = pl.BlockSpec(memory_space=pltpu.VMEM)
    dma = pltpu.SemaphoreType.DMA
    bf16, f32 = jnp.bfloat16, jnp.float32
    return pl.pallas_call(
        kernel,
        out_shape=jax.ShapeDtypeStruct((COUNT, 1024), f32),
        in_specs=[vmem] * 3,
        out_specs=vmem,
        scratch_shapes=[
            pltpu.VMEM((PARTS, SLICE, LANES), bf16),
            pltpu.VMEM((PARTS, SLICE, LANES), bf16),
            pltpu.VMEM((2, PARTS * GROUP, LANES), f32),
            pltpu.VMEM((2, GROUP, LANES), f32),
            pltpu.VMEM((LINE, GROUP, DEPTH), bf16),
            pltpu.VMEM((LINE, ROWS, DEPTH), bf16),
            pltpu.VMEM((LINE, LINE, ROWS, DEPTH), bf16),
            pltpu.VMEM((LINE * GROUP, LINE * GROUP), f32),
            pltpu.VMEM((PARTS, LINE * COUNT, LINE * GROUP), f32),
            pltpu.VMEM((PARTS, LINE * COUNT, LINE * GROUP), f32),
            pltpu.VMEM((LINE, COUNT, LINE * GROUP), f32),
            pltpu.VMEM((LINE, COUNT, LINE * GROUP), f32),
            pltpu.VMEM((LINE * COUNT, LINE * GROUP), f32),
            dma((PARTS,)), dma((PARTS,)),
            dma((LINE,)), dma((LINE,)), dma((LINE,)), dma((LINE,)),
            dma((PARTS,)), dma((PARTS,)),
            dma((LINE,)), dma((LINE,)),
            dma,
        ],
        compiler_params=pltpu.CompilerParams(collective_id=0, has_side_effects=True, vmem_limit_bytes=32 << 20),
        name="schur",
    )(constraint_mats, primal_matrix, inverse_dual_iterate)


def solution(mesh):
    in_specs = (P(("narrow", "wide"), None, None), P(), P())
    out_specs = P(("narrow", "wide"), None)
    return jax.shard_map(body, mesh=mesh, in_specs=in_specs, out_specs=out_specs, check_vma=False)
```

```python
import jax
import jax.numpy as jnp
from jax import lax
from jax.experimental import pallas as pl
from jax.experimental.pallas import tpu as pltpu
from jax.sharding import PartitionSpec as P

PARTS = 16
LINE = 4
COUNT = 4
ROWS = 16
LANES = 128
RING = 8
DEPTH = ROWS * LANES
GROUP = PARTS * COUNT
FAR_FIRST = (4, 3, 5, 2, 6, 1, 7, 0)


def dot(a, b):
    return lax.dot_general(a, b, (((1,), (0,)), ((), ())), preferred_element_type=jnp.float32)


def dot_nt(a, b):
    return lax.dot_general(a, b, (((1,), (1,)), ((), ())), preferred_element_type=jnp.float32)


def pick_lanes(value, pick):
    high = value.astype(jnp.bfloat16)
    rest = value - high.astype(jnp.float32)
    mid = rest.astype(jnp.bfloat16)
    low = (rest - mid.astype(jnp.float32)).astype(jnp.bfloat16)
    return dot(high, pick) + dot(mid, pick) + dot(low, pick)


def kernel(a_hbm, x_hbm, z_hbm, out_ref, mats, primal_ref, dual_ref, send1, recv1, send1_diag, recv1_diag, wide_rows,
           diag_rows, v_all, a_all, v_diag, a_diag, partial, halves, sibling, send3, recv3, joined,
           load, s1, r1, s1d, r1d, s2v, r2v, s2a, r2a, s2vd, r2vd, s2ad, r2ad, sh, rh, s3, r3, own_sem):
    wide, narrow = lax.axis_index("wide"), lax.axis_index("narrow")
    y = lax.rem(wide, 4)
    x = lax.rem(lax.div(wide, 4), 4)
    z_lo = lax.div(wide, 16)
    core = lax.rem(narrow, 2)
    z = lax.div(narrow, 2) * 4 + z_lo
    part = narrow * 4 + z_lo

    def device(x_at, y_at, z_at, core_at):
        return {"wide": lax.rem(z_at, 4) * 16 + x_at * 4 + y_at, "narrow": lax.div(z_at, 4) * 2 + core_at}

    def part_of(z_at, core_at):
        return (lax.div(z_at, 4) * 2 + core_at) * 4 + lax.rem(z_at, 4)

    column = [(lax.rem(z + dz, RING), lax.rem(core + dc, 2)) for dz in FAR_FIRST for dc in (0, 1) if dz or dc]
    owners = [(lax.rem(z + dz, RING), lax.rem(y + dy, LINE)) for dz in FAR_FIRST for dy in (2, 1, 3, 0) if dz or dy]
    line_x = [lax.rem(x + k, LINE) for k in (2, 1, 3)]
    line_y = [lax.rem(y + k, LINE) for k in (2, 1, 3)]

    loads = [pltpu.make_async_copy(x_hbm, primal_ref, load.at[4]), pltpu.make_async_copy(z_hbm, dual_ref, load.at[5])]
    for c in range(COUNT):
        loads.append(pltpu.make_async_copy(a_hbm.at[c], mats.at[c], load.at[c]))
    for copy in loads:
        copy.start()

    barrier = pltpu.get_barrier_semaphore()
    greeted = [device(x, y, z_at, core_at) for z_at, core_at in column]
    greeted += [device(x, y_at, lax.rem(z + dz, RING), core) for dz in FAR_FIRST[:-1] for y_at in line_y]
    greeted += [device(k, y, z, core) for k in line_x] + [device(x, k, z, core) for k in line_y]
    for peer in greeted:
        pl.semaphore_signal(barrier, inc=1, device_id=peer)

    def copy1(c, slot, z_to, core_to):
        to = part_of(z_to, core_to)
        return pltpu.make_async_remote_copy(
            src_ref=send1.at[c, to], dst_ref=recv1.at[c, slot], send_sem=s1.at[c, to], recv_sem=r1.at[c, slot],
            device_id=device(x, y, z_to, core_to),
        )

    def copy1_diag(slot, z_to, core_to):
        to = part_of(z_to, core_to)
        return pltpu.make_async_remote_copy(
            src_ref=send1_diag, dst_ref=recv1_diag.at[slot], send_sem=s1d.at[to], recv_sem=r1d.at[slot],
            device_id=device(x, y, z_to, core_to),
        )

    def own1(c):
        return pltpu.make_async_copy(send1.at[c, part], recv1.at[c, part], own_sem.at[c])

    row = lax.broadcasted_iota(jnp.int32, (LANES, LANES), 0)
    col = lax.broadcasted_iota(jnp.int32, (LANES, LANES), 1)
    loads[0].wait()
    loads[1].wait()
    primal, dual = primal_ref[...], dual_ref[...]
    diag_a, diag_v = [], []
    for c in range(COUNT):
        loads[2 + c].wait()
        mat = mats[c]
        left = dot(primal, mat).astype(jnp.bfloat16)
        top = dot(left[:LANES], dual) + dot_nt(dual[:LANES], left)
        low = dot(left[LANES:], dual[:, LANES:]) + dot_nt(dual[LANES:], left[LANES:])
        mat32 = mat.astype(jnp.float32)
        a_up, a_low = mat32[:LANES, :LANES], mat32[LANES:, LANES:]
        fold_a = [mat[:LANES, LANES:], jnp.where(row <= col, a_up, a_low).astype(jnp.bfloat16)]
        corner = jnp.where(row < col, top[:, :LANES], jnp.where(row == col, 0.5 * top[:, :LANES], low))
        fold_v = [top[:, LANES:].astype(jnp.bfloat16), corner.astype(jnp.bfloat16)]
        diag_a.append(jnp.sum(jnp.where(row == col, a_low, 0.0), axis=0, keepdims=True))
        diag_v.append(jnp.sum(jnp.where(row == col, low, 0.0), axis=0, keepdims=True) * (0.5 / PARTS))
        for d in range(PARTS):
            half, at = d // 8, (d % 8) * ROWS
            send1[c, d, :ROWS, :] = fold_a[half][at:at + ROWS]
            send1[c, d, ROWS:, :] = fold_v[half][at:at + ROWS]
        if c == COUNT - 1:
            send1_diag[...] = jnp.concatenate(diag_a + diag_v, axis=0).astype(jnp.bfloat16)
        if c == 0:
            pl.semaphore_wait(barrier, len(greeted))
        for z_to, core_to in column:
            copy1(c, part, z_to, core_to).start()
            if c == COUNT - 1:
                copy1_diag(part, z_to, core_to).start()
        own1(c).start()
    recv1_diag[part] = send1_diag[...]

    def copy2(ref, slot, c, sems, to):
        along, to = to
        peer = device(x, to, z, core) if along == "y" else device(to, y, z, core)
        at = ref.at[slot, c] if c is not None else ref.at[slot]
        where = (lambda k: (k, c)) if c is not None else (lambda k: (k,))
        return pltpu.make_async_remote_copy(
            src_ref=at, dst_ref=at, send_sem=sems[0].at[where(to)], recv_sem=sems[1].at[where(slot)], device_id=peer
        )

    def lines(c, sending):
        v, a, sv, sa = (v_all, a_all, (s2v, r2v), (s2a, r2a)) if c is not None else (v_diag, a_diag, (s2vd, r2vd), (s2ad, r2ad))
        copies = []
        for ky, kx in zip(line_y, line_x):
            copies.append(copy2(v, y if sending else ky, c, sv, ("y", ky)))
            copies.append(copy2(a, x if sending else kx, c, sa, ("x", kx)))
        return copies

    for c in range(COUNT):
        own1(c).wait()
        for z_from, core_from in reversed(column):
            copy1(c, part_of(z_from, core_from), z_from, core_from).wait_recv()
        for s in range(PARTS):
            block = recv1[c, s].astype(jnp.float32)
            wide_rows[c, 0, ROWS * s:ROWS * (s + 1), :] = block[:ROWS]
            wide_rows[c, 1, ROWS * s:ROWS * (s + 1), :] = block[ROWS:]
        for r in range(ROWS):
            at = pl.ds(r * LANES, LANES)
            a_all[x, c, :, at] = wide_rows[c, 0, pl.ds(r, PARTS, stride=ROWS), :].astype(jnp.bfloat16)
            v_all[y, c, :, at] = wide_rows[c, 1, pl.ds(r, PARTS, stride=ROWS), :].astype(jnp.bfloat16)
        for copy in lines(c, True):
            copy.start()
    for z_from, core_from in reversed(column):
        copy1_diag(part_of(z_from, core_from), z_from, core_from).wait_recv()
    for s in range(PARTS):
        diag_rows[pl.ds(RING * s, RING), :] = recv1_diag[s].astype(jnp.float32)
    for c in range(COUNT):
        at = slice(PARTS * c, PARTS * (c + 1))
        a_diag[x, at, :] = diag_rows[pl.ds(c, PARTS, stride=RING), :].astype(jnp.bfloat16)
        v_diag[y, at, :] = diag_rows[pl.ds(COUNT + c, PARTS, stride=RING), :].astype(jnp.bfloat16)
    for copy in lines(None, True):
        copy.start()
    for c in (*range(COUNT), None):
        for copy in lines(c, False):
            copy.wait_recv()

    size = LINE * GROUP
    product = dot_nt(v_all[...].reshape(size, DEPTH), a_all[...].reshape(size, DEPTH)) + dot_nt(
        v_diag[...].reshape(size, LANES), a_diag[...].reshape(size, LANES)
    )
    for h in range(2):
        partial[h] = product[:, LANES * h:LANES * (h + 1)]

    for core_to in range(2):
        for z_to in range(RING):
            p = (z_to // 4 * 2 + core_to) * 4 + z_to % 4
            for h in range(2):
                halves[core_to, z_to, :, LANES * h:LANES * (h + 1)] = partial[h, pl.ds(p, LINE * COUNT, stride=PARTS), :]
    other = lax.rem(core + 1, 2)
    swap = pltpu.make_async_remote_copy(
        src_ref=halves.at[other], dst_ref=sibling, send_sem=sh, recv_sem=rh, device_id=device(x, y, z, other)
    )
    swap.start()
    swap.wait_recv()
    for z_to in range(RING):
        both = halves[core, z_to] + sibling[z_to]
        for k in range(LINE):
            send3[z_to, k] = both[COUNT * k:COUNT * (k + 1)]

    def copy3(z_slot, y_slot, z_to, y_to):
        return pltpu.make_async_remote_copy(
            src_ref=send3.at[z_to, y_to], dst_ref=recv3.at[z_slot, y_slot], send_sem=s3.at[z_to, y_to],
            recv_sem=r3.at[z_slot, y_slot], device_id=device(x, y_to, z_to, core),
        )

    for z_to, y_to in owners:
        copy3(z, y, z_to, y_to).start()
    recv3[z, y] = send3[z, y]

    lane_from = lax.broadcasted_iota(jnp.int32, (size, size), 0)
    lane_to = lax.broadcasted_iota(jnp.int32, (size, size), 1)
    digit = lambda place: lax.rem(lax.div(lane_to, place), 4)
    first = digit(16) * 64 + digit(1) * 16 + digit(64) * 4 + digit(4)
    second = digit(4) * 64 + digit(16) * 16 + digit(64) * 4 + digit(1)
    pick1 = jnp.where(lane_from == first, 1.0, 0.0).astype(jnp.bfloat16)
    pick2 = jnp.where(lane_from == second, 1.0, 0.0).astype(jnp.bfloat16)

    for z_from, y_from in reversed(owners):
        copy3(z_from, y_from, z_from, y_from).wait_recv()
    rows = []
    for k in range(LINE):
        total = recv3[0, k]
        for z_from in range(1, RING):
            total = total + recv3[z_from, k]
        rows.append(total)
    grouped = pick_lanes(jnp.concatenate(rows, axis=0), pick1)
    for k in range(LINE):
        for n in range(LINE):
            joined[COUNT * n:COUNT * (n + 1), GROUP * k:GROUP * (k + 1)] = grouped[
                COUNT * k:COUNT * (k + 1), GROUP * n:GROUP * (n + 1)
            ]
    ordered = pick_lanes(joined[...], pick2)
    for n in range(LINE):
        out_ref[:, size * n:size * (n + 1)] = ordered[COUNT * n:COUNT * (n + 1)]

    for c in range(COUNT):
        for z_to, core_to in column:
            copy1(c, part, z_to, core_to).wait_send()
    for z_to, core_to in column:
        copy1_diag(part, z_to, core_to).wait_send()
    for c in (*range(COUNT), None):
        for copy in lines(c, True):
            copy.wait_send()
    swap.wait_send()
    for z_to, y_to in owners:
        copy3(z, y, z_to, y_to).wait_send()


def body(constraint_mats, primal_matrix, inverse_dual_iterate):
    hbm = pl.BlockSpec(memory_space=pltpu.HBM)
    dma = pltpu.SemaphoreType.DMA
    bf16, f32 = jnp.bfloat16, jnp.float32
    order = 2 * LANES
    size = LINE * GROUP
    return pl.pallas_call(
        kernel,
        out_shape=jax.ShapeDtypeStruct((COUNT, 1024), f32),
        in_specs=[hbm] * 3,
        out_specs=pl.BlockSpec(memory_space=pltpu.VMEM),
        scratch_shapes=[
            pltpu.VMEM((COUNT, order, order), bf16),
            pltpu.VMEM((order, order), bf16),
            pltpu.VMEM((order, order), bf16),
            pltpu.VMEM((COUNT, PARTS, 2 * ROWS, LANES), bf16),
            pltpu.VMEM((COUNT, PARTS, 2 * ROWS, LANES), bf16),
            pltpu.VMEM((2 * COUNT, LANES), bf16),
            pltpu.VMEM((PARTS, 2 * COUNT, LANES), bf16),
            pltpu.VMEM((COUNT, 2, PARTS * ROWS, LANES), f32),
            pltpu.VMEM((PARTS * 2 * COUNT, LANES), f32),
            pltpu.VMEM((LINE, COUNT, PARTS, DEPTH), bf16),
            pltpu.VMEM((LINE, COUNT, PARTS, DEPTH), bf16),
            pltpu.VMEM((LINE, GROUP, LANES), bf16),
            pltpu.VMEM((LINE, GROUP, LANES), bf16),
            pltpu.VMEM((2, size, LANES), f32),
            pltpu.VMEM((2, RING, LINE * COUNT, size), f32),
            pltpu.VMEM((RING, LINE * COUNT, size), f32),
            pltpu.VMEM((RING, LINE, COUNT, size), f32),
            pltpu.VMEM((RING, LINE, COUNT, size), f32),
            pltpu.VMEM((LINE * COUNT, size), f32),
            dma((6,)),
            dma((COUNT, PARTS)), dma((COUNT, PARTS)), dma((PARTS,)), dma((PARTS,)),
            dma((LINE, COUNT)), dma((LINE, COUNT)), dma((LINE, COUNT)), dma((LINE, COUNT)),
            dma((LINE,)), dma((LINE,)), dma((LINE,)), dma((LINE,)),
            dma, dma,
            dma((RING, LINE)), dma((RING, LINE)),
            dma((COUNT,)),
        ],
        compiler_params=pltpu.CompilerParams(collective_id=0, has_side_effects=True),
        name="schur",
    )(constraint_mats, primal_matrix, inverse_dual_iterate)


def solution(mesh):
    in_specs = (P(("narrow", "wide"), None, None), P(), P())
    out_specs = P(("narrow", "wide"), None)
    return jax.shard_map(body, mesh=mesh, in_specs=in_specs, out_specs=out_specs, check_vma=False)
```

```python
import jax
import jax.numpy as jnp
from jax import lax
from jax.experimental import pallas as pl
from jax.experimental.pallas import tpu as pltpu
from jax.sharding import PartitionSpec as P

PARTS = 16
LINE = 4
COUNT = 4
ROWS = 16
LANES = 128
RING = 8
DEPTH = ROWS * LANES
GROUP = PARTS * COUNT
FAR_FIRST = (4, 3, 5, 2, 6, 1, 7, 0)


def dot(a, b):
    return lax.dot_general(a, b, (((1,), (0,)), ((), ())), preferred_element_type=jnp.float32)


def dot_nt(a, b):
    return lax.dot_general(a, b, (((1,), (1,)), ((), ())), preferred_element_type=jnp.float32)


def pick_lanes(value, pick):
    high = value.astype(jnp.bfloat16)
    rest = value - high.astype(jnp.float32)
    mid = rest.astype(jnp.bfloat16)
    low = (rest - mid.astype(jnp.float32)).astype(jnp.bfloat16)
    return dot(high, pick) + dot(mid, pick) + dot(low, pick)


def kernel(a_hbm, x_hbm, z_hbm, out_ref, mats, primal_ref, dual_ref, send1, recv1, send1_diag, recv1_diag, wide_rows,
           diag_rows, v_all, a_all, v_diag, a_diag, partial, halves, sibling, send3, recv3, joined,
           load, s1, r1, s1d, r1d, s2, r2, s2d, r2d, sh, rh, s3, r3, own_sem):
    loads = [pltpu.make_async_copy(x_hbm, primal_ref, load.at[4]), pltpu.make_async_copy(z_hbm, dual_ref, load.at[5])]
    for c in range(COUNT):
        loads.append(pltpu.make_async_copy(a_hbm.at[c], mats.at[c], load.at[c]))
    for copy in loads:
        copy.start()

    wide, narrow = lax.axis_index("wide"), lax.axis_index("narrow")
    z_hi = lax.div(narrow, 2)
    core = narrow - 2 * z_hi
    z_lo = lax.div(wide, 16)
    plane = wide - 16 * z_lo
    x = lax.div(plane, 4)
    y = plane - 4 * x
    z = z_hi * 4 + z_lo
    part = narrow * 4 + z_lo

    def wrap(value, size):
        return jnp.where(value >= size, value - size, value)

    column, same_core = [], []
    for dz in FAR_FIRST:
        z_at = wrap(z + dz, RING)
        hi = jnp.where(z_at >= 4, 1, 0)
        lo = z_at - 4 * hi
        for other in (0, 1):
            narrow_at = 2 * hi + (1 - core if other else core)
            if dz or other:
                column.append((narrow_at * 4 + lo, {"wide": lo * 16 + plane, "narrow": narrow_at}))
        same_core.append((z_at, lo * 16 + x * 4, 2 * hi + core))
    line_x, line_y = [], []
    for k in (2, 1, 3):
        x_at, y_at = wrap(x + k, LINE), wrap(y + k, LINE)
        line_x.append((x_at, {"wide": z_lo * 16 + x_at * 4 + y, "narrow": narrow}))
        line_y.append((y_at, {"wide": wide - y + y_at, "narrow": narrow}))
    owners = [
        (z_at * LINE + y_at, {"wide": base + y_at, "narrow": narrow_at})
        for z_at, base, narrow_at in same_core[:-1] for y_at in [k for k, _ in line_y] + [y]
    ] + [(z * LINE + y_at, peer) for y_at, peer in line_y]
    sibling_core = {"wide": wide, "narrow": 2 * z_hi + 1 - core}

    barrier = pltpu.get_barrier_semaphore()
    greeted = [peer for _, peer in column + line_x + line_y]
    for peer in greeted:
        pl.semaphore_signal(barrier, inc=1, device_id=peer)

    def remote(src, dst, send_sem, recv_sem, peer):
        return pltpu.make_async_remote_copy(
            src_ref=src, dst_ref=dst, send_sem=send_sem, recv_sem=recv_sem, device_id=peer
        )

    def wait_bytes(like, sem):
        pltpu.make_async_copy(like, like, sem).wait()

    def own1(c):
        return pltpu.make_async_copy(send1.at[c, part], recv1.at[c, part], own_sem.at[c])

    row = lax.broadcasted_iota(jnp.int32, (LANES, LANES), 0)
    col = lax.broadcasted_iota(jnp.int32, (LANES, LANES), 1)
    loads[0].wait()
    loads[1].wait()
    primal, dual = primal_ref[...], dual_ref[...]
    diag_a, diag_v = [], []
    for c in range(COUNT):
        loads[2 + c].wait()
        mat = mats[c]
        left = dot(primal, mat).astype(jnp.bfloat16)
        top = dot(left[:LANES], dual) + dot_nt(dual[:LANES], left)
        low = dot(left[LANES:], dual[:, LANES:]) + dot_nt(dual[LANES:], left[LANES:])
        mat32 = mat.astype(jnp.float32)
        a_up, a_low = mat32[:LANES, :LANES], mat32[LANES:, LANES:]
        fold_a = [mat[:LANES, LANES:], jnp.where(row <= col, a_up, a_low).astype(jnp.bfloat16)]
        corner = jnp.where(row < col, top[:, :LANES], jnp.where(row == col, 0.5 * top[:, :LANES], low))
        fold_v = [top[:, LANES:].astype(jnp.bfloat16), corner.astype(jnp.bfloat16)]
        diag_a.append(jnp.sum(jnp.where(row == col, a_low, 0.0), axis=0, keepdims=True))
        diag_v.append(jnp.sum(jnp.where(row == col, low, 0.0), axis=0, keepdims=True) * (0.5 / PARTS))
        for d in range(PARTS):
            half, at = d // 8, (d % 8) * ROWS
            send1[c, d, :ROWS, :] = fold_a[half][at:at + ROWS]
            send1[c, d, ROWS:, :] = fold_v[half][at:at + ROWS]
        if c == 0:
            pl.semaphore_wait(barrier, len(greeted))
        if c == COUNT - 1:
            send1_diag[...] = jnp.concatenate(diag_a + diag_v, axis=0).astype(jnp.bfloat16)
            for _, peer in column:
                remote(send1_diag, recv1_diag.at[part], s1d, r1d, peer).start()
        for to, peer in column:
            remote(send1.at[c, to], recv1.at[c, part], s1.at[c], r1.at[c], peer).start()
        own1(c).start()
    recv1_diag[part] = send1_diag[...]

    def send_lines(v, a, send_sem, recv_sem):
        for (_, peer_y), (_, peer_x) in zip(line_y, line_x):
            remote(v(y), v(y), send_sem.at[0], recv_sem.at[0], peer_y).start()
            remote(a(x), a(x), send_sem.at[1], recv_sem.at[1], peer_x).start()

    for c in range(COUNT):
        if c == COUNT - 1:
            wait_bytes(recv1_diag.at[:PARTS - 1], r1d)
            for s in range(PARTS):
                diag_rows[pl.ds(RING * s, RING), :] = recv1_diag[s].astype(jnp.float32)
            for k in range(COUNT):
                at = slice(PARTS * k, PARTS * (k + 1))
                a_diag[x, at, :] = diag_rows[pl.ds(k, PARTS, stride=RING), :].astype(jnp.bfloat16)
                v_diag[y, at, :] = diag_rows[pl.ds(COUNT + k, PARTS, stride=RING), :].astype(jnp.bfloat16)
            send_lines(lambda k: v_diag.at[k], lambda k: a_diag.at[k], s2d, r2d)
        own1(c).wait()
        wait_bytes(recv1.at[c, :PARTS - 1], r1.at[c])
        for s in range(PARTS):
            block = recv1[c, s].astype(jnp.float32)
            wide_rows[c, 0, ROWS * s:ROWS * (s + 1), :] = block[:ROWS]
            wide_rows[c, 1, ROWS * s:ROWS * (s + 1), :] = block[ROWS:]
        for r in range(ROWS):
            at = pl.ds(r * LANES, LANES)
            a_all[x, c, :, at] = wide_rows[c, 0, pl.ds(r, PARTS, stride=ROWS), :].astype(jnp.bfloat16)
            v_all[y, c, :, at] = wide_rows[c, 1, pl.ds(r, PARTS, stride=ROWS), :].astype(jnp.bfloat16)
        send_lines(lambda k: v_all.at[k, c], lambda k: a_all.at[k, c], s2, r2)
    for k, (v, a) in enumerate(((v_all, v_diag), (a_all, a_diag))):
        wait_bytes(a.at[:LINE - 1], r2d.at[k])
        wait_bytes(v.at[:LINE - 1], r2.at[k])

    size = LINE * GROUP
    v_mat, v_end = v_all[...].reshape(size, DEPTH), v_diag[...].reshape(size, LANES)
    swaps = []
    for h in range(2):
        a_mat = a_all[2 * h:2 * h + 2].reshape(LANES, DEPTH)
        a_end = a_diag[2 * h:2 * h + 2].reshape(LANES, LANES)
        partial[h] = dot_nt(v_mat, a_mat) + dot_nt(v_end, a_end)
        for core_to in range(2):
            for z_to in range(RING):
                p = (z_to // 4 * 2 + core_to) * 4 + z_to % 4
                halves[core_to, h, z_to] = partial[h, pl.ds(p, LINE * COUNT, stride=PARTS), :]
        swaps.append(remote(halves.at[1 - core, h], sibling.at[h], sh.at[h], rh.at[h], sibling_core))
        swaps[h].start()
    for h in range(2):
        swaps[h].wait_recv()
        for z_to in range(RING):
            both = halves[core, h, z_to] + sibling[h, z_to]
            for k in range(LINE):
                send3[z_to * LINE + k, :, LANES * h:LANES * (h + 1)] = both[COUNT * k:COUNT * (k + 1)]
    own = z * LINE + y
    for to, peer in owners:
        remote(send3.at[to], recv3.at[own], s3, r3, peer).start()
    recv3[own] = send3[own]

    lane_from = lax.broadcasted_iota(jnp.int32, (size, size), 0)
    lane_to = lax.broadcasted_iota(jnp.int32, (size, size), 1)
    digit = lambda place: lax.rem(lax.div(lane_to, place), 4)
    first = digit(16) * 64 + digit(1) * 16 + digit(64) * 4 + digit(4)
    second = digit(4) * 64 + digit(16) * 16 + digit(64) * 4 + digit(1)
    pick1 = jnp.where(lane_from == first, 1.0, 0.0).astype(jnp.bfloat16)
    pick2 = jnp.where(lane_from == second, 1.0, 0.0).astype(jnp.bfloat16)

    wait_bytes(recv3.at[:RING * LINE - 1], r3)
    rows = []
    for k in range(LINE):
        total = recv3[k]
        for z_from in range(1, RING):
            total = total + recv3[z_from * LINE + k]
        rows.append(total)
    grouped = pick_lanes(jnp.concatenate(rows, axis=0), pick1)
    for k in range(LINE):
        for n in range(LINE):
            joined[COUNT * n:COUNT * (n + 1), GROUP * k:GROUP * (k + 1)] = grouped[
                COUNT * k:COUNT * (k + 1), GROUP * n:GROUP * (n + 1)
            ]
    ordered = pick_lanes(joined[...], pick2)
    for n in range(LINE):
        out_ref[:, size * n:size * (n + 1)] = ordered[COUNT * n:COUNT * (n + 1)]

    for c in range(COUNT):
        wait_bytes(recv1.at[c, :PARTS - 1], s1.at[c])
    wait_bytes(recv1_diag.at[:PARTS - 1], s1d)
    for k in range(2):
        wait_bytes(v_all.at[:LINE - 1], s2.at[k])
        wait_bytes(v_diag.at[:LINE - 1], s2d.at[k])
        swaps[k].wait_send()
    wait_bytes(recv3.at[:RING * LINE - 1], s3)


def body(constraint_mats, primal_matrix, inverse_dual_iterate):
    hbm = pl.BlockSpec(memory_space=pltpu.HBM)
    dma = pltpu.SemaphoreType.DMA
    bf16, f32 = jnp.bfloat16, jnp.float32
    order = 2 * LANES
    size = LINE * GROUP
    return pl.pallas_call(
        kernel,
        out_shape=jax.ShapeDtypeStruct((COUNT, 1024), f32),
        in_specs=[hbm] * 3,
        out_specs=pl.BlockSpec(memory_space=pltpu.VMEM),
        scratch_shapes=[
            pltpu.VMEM((COUNT, order, order), bf16),
            pltpu.VMEM((order, order), bf16),
            pltpu.VMEM((order, order), bf16),
            pltpu.VMEM((COUNT, PARTS, 2 * ROWS, LANES), bf16),
            pltpu.VMEM((COUNT, PARTS, 2 * ROWS, LANES), bf16),
            pltpu.VMEM((2 * COUNT, LANES), bf16),
            pltpu.VMEM((PARTS, 2 * COUNT, LANES), bf16),
            pltpu.VMEM((COUNT, 2, PARTS * ROWS, LANES), f32),
            pltpu.VMEM((PARTS * 2 * COUNT, LANES), f32),
            pltpu.VMEM((LINE, COUNT, PARTS, DEPTH), bf16),
            pltpu.VMEM((LINE, COUNT, PARTS, DEPTH), bf16),
            pltpu.VMEM((LINE, GROUP, LANES), bf16),
            pltpu.VMEM((LINE, GROUP, LANES), bf16),
            pltpu.VMEM((2, size, LANES), f32),
            pltpu.VMEM((2, 2, RING, LINE * COUNT, LANES), f32),
            pltpu.VMEM((2, RING, LINE * COUNT, LANES), f32),
            pltpu.VMEM((RING * LINE, COUNT, size), f32),
            pltpu.VMEM((RING * LINE, COUNT, size), f32),
            pltpu.VMEM((LINE * COUNT, size), f32),
            dma((6,)),
            dma((COUNT,)), dma((COUNT,)), dma, dma,
            dma((2,)), dma((2,)), dma((2,)), dma((2,)),
            dma((2,)), dma((2,)), dma, dma,
            dma((COUNT,)),
        ],
        compiler_params=pltpu.CompilerParams(collective_id=0, has_side_effects=True),
        name="schur",
    )(constraint_mats, primal_matrix, inverse_dual_iterate)


def solution(mesh):
    in_specs = (P(("narrow", "wide"), None, None), P(), P())
    out_specs = P(("narrow", "wide"), None)
    return jax.shard_map(body, mesh=mesh, in_specs=in_specs, out_specs=out_specs, check_vma=False)
```

```python
import jax
import jax.numpy as jnp
from jax import lax
from jax.experimental import pallas as pl
from jax.experimental.pallas import tpu as pltpu
from jax.sharding import PartitionSpec as P

PARTS = 16
LINE = 4
COUNT = 4
ROWS = 16
LANES = 128
RING = 8
DEPTH = ROWS * LANES
GROUP = PARTS * COUNT
FAR_FIRST = (4, 3, 5, 2, 6, 1, 7, 0)


def dot(a, b):
    return lax.dot_general(a, b, (((1,), (0,)), ((), ())), preferred_element_type=jnp.float32)


def dot_nt(a, b):
    return lax.dot_general(a, b, (((1,), (1,)), ((), ())), preferred_element_type=jnp.float32)


def pick_lanes(value, pick):
    high = value.astype(jnp.bfloat16)
    rest = value - high.astype(jnp.float32)
    mid = rest.astype(jnp.bfloat16)
    low = (rest - mid.astype(jnp.float32)).astype(jnp.bfloat16)
    return dot(high, pick) + dot(mid, pick) + dot(low, pick)


def kernel(a_hbm, x_hbm, z_hbm, out_ref, mats, primal_ref, dual_ref, send1, recv1, send1_diag, recv1_diag, wide_rows,
           diag_rows, v_all, a_all, v_diag, a_diag, partial, halves, sibling, send3, recv3, joined,
           load, s1, r1, s1d, r1d, s2, r2, sf, rf, s2d, r2d, sh, rh, s3, r3, own_sem):
    loads = [pltpu.make_async_copy(x_hbm, primal_ref, load.at[4]), pltpu.make_async_copy(z_hbm, dual_ref, load.at[5])]
    for c in range(COUNT):
        loads.append(pltpu.make_async_copy(a_hbm.at[c], mats.at[c], load.at[c]))
    for copy in loads:
        copy.start()

    wide, narrow = lax.axis_index("wide"), lax.axis_index("narrow")
    z_hi = lax.div(narrow, 2)
    core = narrow - 2 * z_hi
    z_lo = lax.div(wide, 16)
    plane = wide - 16 * z_lo
    x = lax.div(plane, 4)
    y = plane - 4 * x
    z = z_hi * 4 + z_lo
    part = narrow * 4 + z_lo

    def wrap(value, size):
        return jnp.where(value >= size, value - size, value)

    column, same_core = [], []
    for dz in FAR_FIRST:
        z_at = wrap(z + dz, RING)
        hi = jnp.where(z_at >= 4, 1, 0)
        lo = z_at - 4 * hi
        for other in (0, 1):
            narrow_at = 2 * hi + (1 - core if other else core)
            if dz or other:
                column.append((narrow_at * 4 + lo, {"wide": lo * 16 + plane, "narrow": narrow_at}))
        same_core.append((z_at, lo * 16 + x * 4, 2 * hi + core))
    line_x, line_y = [], []
    for k in (2, 1, 3):
        x_at, y_at = wrap(x + k, LINE), wrap(y + k, LINE)
        line_x.append((x_at, {"wide": z_lo * 16 + x_at * 4 + y, "narrow": narrow}))
        line_y.append((y_at, {"wide": wide - y + y_at, "narrow": narrow}))
    owners = [
        (z_at * LINE + y_at, {"wide": base + y_at, "narrow": narrow_at})
        for z_at, base, narrow_at in same_core[:-1] for y_at in [k for k, _ in line_y] + [y]
    ] + [(z * LINE + y_at, peer) for y_at, peer in line_y]
    sibling_core = {"wide": wide, "narrow": 2 * z_hi + 1 - core}

    barrier = pltpu.get_barrier_semaphore()
    greeted = [peer for _, peer in column + line_x + line_y]
    for peer in greeted:
        pl.semaphore_signal(barrier, inc=1, device_id=peer)

    def remote(src, dst, send_sem, recv_sem, peer):
        return pltpu.make_async_remote_copy(
            src_ref=src, dst_ref=dst, send_sem=send_sem, recv_sem=recv_sem, device_id=peer
        )

    def wait_bytes(like, sem):
        pltpu.make_async_copy(like, like, sem).wait()

    def own1(c):
        return pltpu.make_async_copy(send1.at[c, part], recv1.at[c, part], own_sem.at[c])

    row = lax.broadcasted_iota(jnp.int32, (LANES, LANES), 0)
    col = lax.broadcasted_iota(jnp.int32, (LANES, LANES), 1)
    loads[0].wait()
    loads[1].wait()
    primal, dual = primal_ref[...], dual_ref[...]
    diag_a, diag_v = [], []
    for c in range(COUNT):
        loads[2 + c].wait()
        mat = mats[c]
        left = dot(primal, mat).astype(jnp.bfloat16)
        top = dot(left[:LANES], dual) + dot_nt(dual[:LANES], left)
        low = dot(left[LANES:], dual[:, LANES:]) + dot_nt(dual[LANES:], left[LANES:])
        mat32 = mat.astype(jnp.float32)
        a_up, a_low = mat32[:LANES, :LANES], mat32[LANES:, LANES:]
        fold_a = [mat[:LANES, LANES:], jnp.where(row <= col, a_up, a_low).astype(jnp.bfloat16)]
        corner = jnp.where(row < col, top[:, :LANES], jnp.where(row == col, 0.5 * top[:, :LANES], low))
        fold_v = [top[:, LANES:].astype(jnp.bfloat16), corner.astype(jnp.bfloat16)]
        diag_a.append(jnp.sum(jnp.where(row == col, a_low, 0.0), axis=0, keepdims=True))
        diag_v.append(jnp.sum(jnp.where(row == col, low, 0.0), axis=0, keepdims=True) * (0.5 / PARTS))
        for d in range(PARTS):
            half, at = d // 8, (d % 8) * ROWS
            send1[c, d, :ROWS, :] = fold_a[half][at:at + ROWS]
            send1[c, d, ROWS:, :] = fold_v[half][at:at + ROWS]
        if c == 0:
            pl.semaphore_wait(barrier, len(greeted))
        if c == COUNT - 1:
            send1_diag[...] = jnp.concatenate(diag_a + diag_v, axis=0).astype(jnp.bfloat16)
            for _, peer in column:
                remote(send1_diag, recv1_diag.at[part], s1d, r1d, peer).start()
        for to, peer in column:
            remote(send1.at[c, to], recv1.at[c, part], s1.at[c], r1.at[c], peer).start()
        own1(c).start()
    recv1_diag[part] = send1_diag[...]

    axes = ((v_all, v_diag, y, line_y), (a_all, a_diag, x, line_x))
    lanes = (slice(0, DEPTH // 2), slice(DEPTH // 2, DEPTH))

    def send_neighbours(c):
        for k, (ref, _, me, line) in enumerate(axes):
            for _, peer in line[1:]:
                remote(ref.at[me, c], ref.at[me, c], s2.at[k], r2.at[c, k], peer).start()

    def forward(c):
        for k, (ref, _, _, line) in enumerate(axes):
            wait_bytes(ref.at[:2, c], r2.at[c, k])
            for (source, _), (_, peer), half in zip(line[1:], reversed(line[1:]), lanes):
                at = ref.at[source, c, :, half]
                remote(at, at, sf.at[k], rf.at[k], peer).start()

    for c in range(COUNT):
        if c == COUNT - 1:
            wait_bytes(recv1_diag.at[:PARTS - 1], r1d)
            for s in range(PARTS):
                diag_rows[pl.ds(RING * s, RING), :] = recv1_diag[s].astype(jnp.float32)
            for k in range(COUNT):
                at = slice(PARTS * k, PARTS * (k + 1))
                a_diag[x, at, :] = diag_rows[pl.ds(k, PARTS, stride=RING), :].astype(jnp.bfloat16)
                v_diag[y, at, :] = diag_rows[pl.ds(COUNT + k, PARTS, stride=RING), :].astype(jnp.bfloat16)
            for k, (_, ref, me, line) in enumerate(axes):
                for _, peer in line:
                    remote(ref.at[me], ref.at[me], s2d.at[k], r2d.at[k], peer).start()
        own1(c).wait()
        wait_bytes(recv1.at[c, :PARTS - 1], r1.at[c])
        for s in range(PARTS):
            block = recv1[c, s].astype(jnp.float32)
            wide_rows[c, 0, ROWS * s:ROWS * (s + 1), :] = block[:ROWS]
            wide_rows[c, 1, ROWS * s:ROWS * (s + 1), :] = block[ROWS:]
        for r in range(ROWS):
            at = pl.ds(r * LANES, LANES)
            a_all[x, c, :, at] = wide_rows[c, 0, pl.ds(r, PARTS, stride=ROWS), :].astype(jnp.bfloat16)
            v_all[y, c, :, at] = wide_rows[c, 1, pl.ds(r, PARTS, stride=ROWS), :].astype(jnp.bfloat16)
        send_neighbours(c)
        if c:
            forward(c - 1)
    forward(COUNT - 1)
    for k, (ref, ref_diag, _, _) in enumerate(axes):
        wait_bytes(ref_diag.at[:LINE - 1], r2d.at[k])
        wait_bytes(ref.at[0], rf.at[k])

    size = LINE * GROUP
    v_mat, v_end = v_all[...].reshape(size, DEPTH), v_diag[...].reshape(size, LANES)
    product = dot_nt(v_mat, a_all[...].reshape(size, DEPTH)) + dot_nt(v_end, a_diag[...].reshape(size, LANES))
    swaps = []
    for h in range(2):
        partial[h] = product[:, LANES * h:LANES * (h + 1)]
        for core_to in range(2):
            for z_to in range(RING):
                p = (z_to // 4 * 2 + core_to) * 4 + z_to % 4
                halves[core_to, h, z_to] = partial[h, pl.ds(p, LINE * COUNT, stride=PARTS), :]
        swaps.append(remote(halves.at[1 - core, h], sibling.at[h], sh.at[h], rh.at[h], sibling_core))
        swaps[h].start()
    for h in range(2):
        swaps[h].wait_recv()
        for z_to in range(RING):
            both = halves[core, h, z_to] + sibling[h, z_to]
            for k in range(LINE):
                send3[z_to * LINE + k, :, LANES * h:LANES * (h + 1)] = both[COUNT * k:COUNT * (k + 1)]
    own = z * LINE + y
    for to, peer in owners:
        remote(send3.at[to], recv3.at[own], s3, r3, peer).start()
    recv3[own] = send3[own]

    lane_from = lax.broadcasted_iota(jnp.int32, (size, size), 0)
    lane_to = lax.broadcasted_iota(jnp.int32, (size, size), 1)
    digit = lambda place: lax.rem(lax.div(lane_to, place), 4)
    first = digit(16) * 64 + digit(1) * 16 + digit(64) * 4 + digit(4)
    second = digit(4) * 64 + digit(16) * 16 + digit(64) * 4 + digit(1)
    pick1 = jnp.where(lane_from == first, 1.0, 0.0).astype(jnp.bfloat16)
    pick2 = jnp.where(lane_from == second, 1.0, 0.0).astype(jnp.bfloat16)

    wait_bytes(recv3.at[:RING * LINE - 1], r3)
    rows = []
    for k in range(LINE):
        total = recv3[k]
        for z_from in range(1, RING):
            total = total + recv3[z_from * LINE + k]
        rows.append(total)
    grouped = pick_lanes(jnp.concatenate(rows, axis=0), pick1)
    for k in range(LINE):
        for n in range(LINE):
            joined[COUNT * n:COUNT * (n + 1), GROUP * k:GROUP * (k + 1)] = grouped[
                COUNT * k:COUNT * (k + 1), GROUP * n:GROUP * (n + 1)
            ]
    ordered = pick_lanes(joined[...], pick2)
    for n in range(LINE):
        out_ref[:, size * n:size * (n + 1)] = ordered[COUNT * n:COUNT * (n + 1)]

    for c in range(COUNT):
        wait_bytes(recv1.at[c, :PARTS - 1], s1.at[c])
    wait_bytes(recv1_diag.at[:PARTS - 1], s1d)
    for k in range(2):
        wait_bytes(v_all.at[:2], s2.at[k])
        wait_bytes(v_all.at[0], sf.at[k])
        wait_bytes(v_diag.at[:LINE - 1], s2d.at[k])
        swaps[k].wait_send()
    wait_bytes(recv3.at[:RING * LINE - 1], s3)


def body(constraint_mats, primal_matrix, inverse_dual_iterate):
    hbm = pl.BlockSpec(memory_space=pltpu.HBM)
    dma = pltpu.SemaphoreType.DMA
    bf16, f32 = jnp.bfloat16, jnp.float32
    order = 2 * LANES
    size = LINE * GROUP
    return pl.pallas_call(
        kernel,
        out_shape=jax.ShapeDtypeStruct((COUNT, 1024), f32),
        in_specs=[hbm] * 3,
        out_specs=pl.BlockSpec(memory_space=pltpu.VMEM),
        scratch_shapes=[
            pltpu.VMEM((COUNT, order, order), bf16),
            pltpu.VMEM((order, order), bf16),
            pltpu.VMEM((order, order), bf16),
            pltpu.VMEM((COUNT, PARTS, 2 * ROWS, LANES), bf16),
            pltpu.VMEM((COUNT, PARTS, 2 * ROWS, LANES), bf16),
            pltpu.VMEM((2 * COUNT, LANES), bf16),
            pltpu.VMEM((PARTS, 2 * COUNT, LANES), bf16),
            pltpu.VMEM((COUNT, 2, PARTS * ROWS, LANES), f32),
            pltpu.VMEM((PARTS * 2 * COUNT, LANES), f32),
            pltpu.VMEM((LINE, COUNT, PARTS, DEPTH), bf16),
            pltpu.VMEM((LINE, COUNT, PARTS, DEPTH), bf16),
            pltpu.VMEM((LINE, GROUP, LANES), bf16),
            pltpu.VMEM((LINE, GROUP, LANES), bf16),
            pltpu.VMEM((2, size, LANES), f32),
            pltpu.VMEM((2, 2, RING, LINE * COUNT, LANES), f32),
            pltpu.VMEM((2, RING, LINE * COUNT, LANES), f32),
            pltpu.VMEM((RING * LINE, COUNT, size), f32),
            pltpu.VMEM((RING * LINE, COUNT, size), f32),
            pltpu.VMEM((LINE * COUNT, size), f32),
            dma((6,)),
            dma((COUNT,)), dma((COUNT,)), dma, dma,
            dma((2,)), dma((COUNT, 2)), dma((2,)), dma((2,)), dma((2,)), dma((2,)),
            dma((2,)), dma((2,)), dma, dma,
            dma((COUNT,)),
        ],
        compiler_params=pltpu.CompilerParams(collective_id=0, has_side_effects=True),
        name="schur",
    )(constraint_mats, primal_matrix, inverse_dual_iterate)


def solution(mesh):
    in_specs = (P(("narrow", "wide"), None, None), P(), P())
    out_specs = P(("narrow", "wide"), None)
    return jax.shard_map(body, mesh=mesh, in_specs=in_specs, out_specs=out_specs, check_vma=False)
```

```python
import jax
import jax.numpy as jnp
from jax import lax
from jax.experimental import pallas as pl
from jax.experimental.pallas import tpu as pltpu
from jax.sharding import PartitionSpec as P

PARTS = 16
LINE = 4
COUNT = 4
ROWS = 16
LANES = 128
RING = 8
DEPTH = ROWS * LANES
GROUP = PARTS * COUNT
FAR_FIRST = (4, 3, 5, 2, 6, 1, 7, 0)
CHUNKS = ((0, 0, 16), (1, 0, 16), (2, 0, 16), (3, 0, 8), (3, 8, 16))
FORWARDED = 3


def dot(a, b):
    return lax.dot_general(a, b, (((1,), (0,)), ((), ())), preferred_element_type=jnp.float32)


def dot_nt(a, b):
    return lax.dot_general(a, b, (((1,), (1,)), ((), ())), preferred_element_type=jnp.float32)


def pick_lanes(value, pick):
    high = value.astype(jnp.bfloat16)
    rest = value - high.astype(jnp.float32)
    mid = rest.astype(jnp.bfloat16)
    low = (rest - mid.astype(jnp.float32)).astype(jnp.bfloat16)
    return dot(high, pick) + dot(mid, pick) + dot(low, pick)


def kernel(a_hbm, x_hbm, z_hbm, out_ref, mats, primal_ref, dual_ref, send1, recv1, send1_diag, recv1_diag, wide_rows,
           diag_rows, v_all, a_all, v_diag, a_diag, partial, halves, sibling, send3, recv3, joined,
           load, s1, r1, s1d, r1d, s2, r2, sf, rf, s2d, r2d, sh, rh, s3, r3, own_sem):
    loads = [pltpu.make_async_copy(x_hbm, primal_ref, load.at[4]), pltpu.make_async_copy(z_hbm, dual_ref, load.at[5])]
    for c in range(COUNT):
        loads.append(pltpu.make_async_copy(a_hbm.at[c], mats.at[c], load.at[c]))
    for copy in loads:
        copy.start()

    wide, narrow = lax.axis_index("wide"), lax.axis_index("narrow")
    z_hi = lax.div(narrow, 2)
    core = narrow - 2 * z_hi
    z_lo = lax.div(wide, 16)
    plane = wide - 16 * z_lo
    x = lax.div(plane, 4)
    y = plane - 4 * x
    z = z_hi * 4 + z_lo
    part = narrow * 4 + z_lo

    def wrap(value, size):
        return jnp.where(value >= size, value - size, value)

    column, same_core = [], []
    for dz in FAR_FIRST:
        z_at = wrap(z + dz, RING)
        hi = jnp.where(z_at >= 4, 1, 0)
        lo = z_at - 4 * hi
        for other in (0, 1):
            narrow_at = 2 * hi + (1 - core if other else core)
            if dz or other:
                column.append((narrow_at * 4 + lo, {"wide": lo * 16 + plane, "narrow": narrow_at}))
        same_core.append((z_at, lo * 16 + x * 4, 2 * hi + core))
    line_x, line_y = [], []
    for k in (2, 1, 3):
        x_at, y_at = wrap(x + k, LINE), wrap(y + k, LINE)
        line_x.append((x_at, {"wide": z_lo * 16 + x_at * 4 + y, "narrow": narrow}))
        line_y.append((y_at, {"wide": wide - y + y_at, "narrow": narrow}))
    sibling_core = {"wide": wide, "narrow": 2 * z_hi + 1 - core}

    barrier = pltpu.get_barrier_semaphore()
    greeted = [peer for _, peer in column + line_x + line_y]
    for peer in greeted:
        pl.semaphore_signal(barrier, inc=1, device_id=peer)

    def remote(src, dst, send_sem, recv_sem, peer):
        return pltpu.make_async_remote_copy(
            src_ref=src, dst_ref=dst, send_sem=send_sem, recv_sem=recv_sem, device_id=peer
        )

    def wait_bytes(like, sem):
        pltpu.make_async_copy(like, like, sem).wait()

    def rows_of(k):
        c, start, stop = CHUNKS[k]
        return c, slice(2 * start, 2 * stop)

    def own1(k):
        c, rows = rows_of(k)
        return pltpu.make_async_copy(send1.at[c, part, rows], recv1.at[c, part, rows], own_sem.at[k])

    row = lax.broadcasted_iota(jnp.int32, (LANES, LANES), 0)
    col = lax.broadcasted_iota(jnp.int32, (LANES, LANES), 1)
    loads[0].wait()
    loads[1].wait()
    primal, dual = primal_ref[...], dual_ref[...]
    diag_a, diag_v = [], []
    for c in range(COUNT):
        loads[2 + c].wait()
        mat = mats[c]
        left = dot(primal, mat).astype(jnp.bfloat16)
        top = dot(left[:LANES], dual) + dot_nt(dual[:LANES], left)
        low = dot(left[LANES:], dual[:, LANES:]) + dot_nt(dual[LANES:], left[LANES:])
        mat32 = mat.astype(jnp.float32)
        a_up, a_low = mat32[:LANES, :LANES], mat32[LANES:, LANES:]
        fold_a = [mat[:LANES, LANES:], jnp.where(row <= col, a_up, a_low).astype(jnp.bfloat16)]
        corner = jnp.where(row < col, top[:, :LANES], jnp.where(row == col, 0.5 * top[:, :LANES], low))
        fold_v = [top[:, LANES:].astype(jnp.bfloat16), corner.astype(jnp.bfloat16)]
        diag_a.append(jnp.sum(jnp.where(row == col, a_low, 0.0), axis=0, keepdims=True))
        diag_v.append(jnp.sum(jnp.where(row == col, low, 0.0), axis=0, keepdims=True) * (0.5 / PARTS))
        for d in range(PARTS):
            half, at = d // 8, (d % 8) * ROWS
            for _, start, stop in [chunk for chunk in CHUNKS if chunk[0] == c]:
                send1[c, d, 2 * start:start + stop, :] = fold_a[half][at + start:at + stop]
                send1[c, d, start + stop:2 * stop, :] = fold_v[half][at + start:at + stop]
        if c == 0:
            pl.semaphore_wait(barrier, len(greeted))
        if c == COUNT - 1:
            send1_diag[...] = jnp.concatenate(diag_a + diag_v, axis=0).astype(jnp.bfloat16)
            for _, peer in column:
                remote(send1_diag, recv1_diag.at[part], s1d, r1d, peer).start()
        for k, chunk in enumerate(CHUNKS):
            if chunk[0] == c:
                _, rows = rows_of(k)
                for to, peer in column:
                    remote(send1.at[c, to, rows], recv1.at[c, part, rows], s1.at[k], r1.at[k], peer).start()
                own1(k).start()
    recv1_diag[part] = send1_diag[...]

    axes = ((v_all, v_diag, y, line_y), (a_all, a_diag, x, line_x))

    def lanes_of(k):
        _, start, stop = CHUNKS[k]
        return slice(start * LANES, stop * LANES)

    def send_lines(k):
        for axis, (ref, _, me, line) in enumerate(axes):
            at = ref.at[me, CHUNKS[k][0], :, lanes_of(k)]
            for _, peer in line[1 if k < FORWARDED else 0:]:
                remote(at, at, s2.at[k, axis], r2.at[k, axis], peer).start()

    def forward(k):
        c = CHUNKS[k][0]
        for axis, (ref, _, _, line) in enumerate(axes):
            wait_bytes(ref.at[:2, c], r2.at[k, axis])
            for half, (source, _), (_, peer) in zip(range(2), line[1:], reversed(line[1:])):
                at = ref.at[source, c, :, half * (DEPTH // 2):(half + 1) * (DEPTH // 2)]
                remote(at, at, sf.at[axis], rf.at[axis], peer).start()

    for k, (c, start, stop) in enumerate(CHUNKS):
        if k == FORWARDED:
            wait_bytes(recv1_diag.at[:PARTS - 1], r1d)
            for s in range(PARTS):
                diag_rows[pl.ds(RING * s, RING), :] = recv1_diag[s].astype(jnp.float32)
            for i in range(COUNT):
                at = slice(PARTS * i, PARTS * (i + 1))
                a_diag[x, at, :] = diag_rows[pl.ds(i, PARTS, stride=RING), :].astype(jnp.bfloat16)
                v_diag[y, at, :] = diag_rows[pl.ds(COUNT + i, PARTS, stride=RING), :].astype(jnp.bfloat16)
            for axis, (_, ref, me, line) in enumerate(axes):
                for _, peer in line:
                    remote(ref.at[me], ref.at[me], s2d.at[axis], r2d.at[axis], peer).start()
        size = stop - start
        own1(k).wait()
        wait_bytes(recv1.at[c, :PARTS - 1, rows_of(k)[1]], r1.at[k])
        for s in range(PARTS):
            block = recv1[c, s, 2 * start:2 * stop, :].astype(jnp.float32)
            wide_rows[k, 0, size * s:size * (s + 1), :] = block[:size]
            wide_rows[k, 1, size * s:size * (s + 1), :] = block[size:]
        for r in range(size):
            at = pl.ds((start + r) * LANES, LANES)
            a_all[x, c, :, at] = wide_rows[k, 0, pl.ds(r, PARTS, stride=size), :].astype(jnp.bfloat16)
            v_all[y, c, :, at] = wide_rows[k, 1, pl.ds(r, PARTS, stride=size), :].astype(jnp.bfloat16)
        send_lines(k)
        if 0 < k <= FORWARDED:
            forward(k - 1)
    for axis, (ref, ref_diag, _, _) in enumerate(axes):
        wait_bytes(ref_diag.at[:LINE - 1], r2d.at[axis])
        wait_bytes(ref.at[0, :FORWARDED], rf.at[axis])
        for k in range(FORWARDED, len(CHUNKS)):
            wait_bytes(ref.at[:LINE - 1, CHUNKS[k][0], :, lanes_of(k)], r2.at[k, axis])

    size = LINE * GROUP
    v_mat, v_end = v_all[...].reshape(size, DEPTH), v_diag[...].reshape(size, LANES)
    product = dot_nt(v_mat, a_all[...].reshape(size, DEPTH)) + dot_nt(v_end, a_diag[...].reshape(size, LANES))
    for h in range(2):
        partial[h] = product[:, LANES * h:LANES * (h + 1)]

    def rows_for(owner, h):
        return partial[h, pl.ds(owner, LINE * COUNT, stride=PARTS), :]

    swaps = []
    for i, (z_at, base, narrow_at) in enumerate(same_core):
        lo = jnp.where(z_at >= 4, z_at - 4, z_at)
        for h in range(2):
            halves[i, h] = rows_for((narrow_at + 1 - 2 * core) * 4 + lo, h)
        swaps.append(remote(halves.at[i], sibling.at[i], sh.at[i], rh.at[i], sibling_core))
        swaps[i].start()
    own = z * LINE + y
    for i, (z_at, base, narrow_at) in enumerate(same_core):
        lo = jnp.where(z_at >= 4, z_at - 4, z_at)
        swaps[i].wait_recv()
        for h in range(2):
            both = rows_for(narrow_at * 4 + lo, h) + sibling[i, h]
            for k in range(LINE):
                send3[z_at * LINE + k, :, LANES * h:LANES * (h + 1)] = both[COUNT * k:COUNT * (k + 1)]
        for y_at, _ in line_y:
            peer = {"wide": base + y_at, "narrow": narrow_at}
            remote(send3.at[z_at * LINE + y_at], recv3.at[own], s3, r3, peer).start()
        if i < RING - 1:
            peer = {"wide": base + y, "narrow": narrow_at}
            remote(send3.at[z_at * LINE + y], recv3.at[own], s3, r3, peer).start()
    recv3[own] = send3[own]

    lane_from = lax.broadcasted_iota(jnp.int32, (size, size), 0)
    lane_to = lax.broadcasted_iota(jnp.int32, (size, size), 1)
    digit = lambda place: lax.rem(lax.div(lane_to, place), 4)
    first = digit(16) * 64 + digit(1) * 16 + digit(64) * 4 + digit(4)
    second = digit(4) * 64 + digit(16) * 16 + digit(64) * 4 + digit(1)
    pick1 = jnp.where(lane_from == first, 1.0, 0.0).astype(jnp.bfloat16)
    pick2 = jnp.where(lane_from == second, 1.0, 0.0).astype(jnp.bfloat16)

    wait_bytes(recv3.at[:RING * LINE - 1], r3)
    rows = []
    for k in range(LINE):
        total = recv3[k]
        for z_from in range(1, RING):
            total = total + recv3[z_from * LINE + k]
        rows.append(total)
    grouped = pick_lanes(jnp.concatenate(rows, axis=0), pick1)
    for k in range(LINE):
        for n in range(LINE):
            joined[COUNT * n:COUNT * (n + 1), GROUP * k:GROUP * (k + 1)] = grouped[
                COUNT * k:COUNT * (k + 1), GROUP * n:GROUP * (n + 1)
            ]
    ordered = pick_lanes(joined[...], pick2)
    for n in range(LINE):
        out_ref[:, size * n:size * (n + 1)] = ordered[COUNT * n:COUNT * (n + 1)]

    for k, (c, _, _) in enumerate(CHUNKS):
        wait_bytes(recv1.at[c, :PARTS - 1, rows_of(k)[1]], s1.at[k])
        for axis in range(2):
            wait_bytes(v_all.at[:2 if k < FORWARDED else LINE - 1, c, :, lanes_of(k)], s2.at[k, axis])
    wait_bytes(recv1_diag.at[:PARTS - 1], s1d)
    for axis in range(2):
        wait_bytes(v_all.at[0, :FORWARDED], sf.at[axis])
        wait_bytes(v_diag.at[:LINE - 1], s2d.at[axis])
    for swap in swaps:
        swap.wait_send()
    wait_bytes(recv3.at[:RING * LINE - 1], s3)


def body(constraint_mats, primal_matrix, inverse_dual_iterate):
    hbm = pl.BlockSpec(memory_space=pltpu.HBM)
    dma = pltpu.SemaphoreType.DMA
    bf16, f32 = jnp.bfloat16, jnp.float32
    order = 2 * LANES
    size = LINE * GROUP
    return pl.pallas_call(
        kernel,
        out_shape=jax.ShapeDtypeStruct((COUNT, 1024), f32),
        in_specs=[hbm] * 3,
        out_specs=pl.BlockSpec(memory_space=pltpu.VMEM),
        scratch_shapes=[
            pltpu.VMEM((COUNT, order, order), bf16),
            pltpu.VMEM((order, order), bf16),
            pltpu.VMEM((order, order), bf16),
            pltpu.VMEM((COUNT, PARTS, 2 * ROWS, LANES), bf16),
            pltpu.VMEM((COUNT, PARTS, 2 * ROWS, LANES), bf16),
            pltpu.VMEM((2 * COUNT, LANES), bf16),
            pltpu.VMEM((PARTS, 2 * COUNT, LANES), bf16),
            pltpu.VMEM((len(CHUNKS), 2, PARTS * ROWS, LANES), f32),
            pltpu.VMEM((PARTS * 2 * COUNT, LANES), f32),
            pltpu.VMEM((LINE, COUNT, PARTS, DEPTH), bf16),
            pltpu.VMEM((LINE, COUNT, PARTS, DEPTH), bf16),
            pltpu.VMEM((LINE, GROUP, LANES), bf16),
            pltpu.VMEM((LINE, GROUP, LANES), bf16),
            pltpu.VMEM((2, size, LANES), f32),
            pltpu.VMEM((RING, 2, LINE * COUNT, LANES), f32),
            pltpu.VMEM((RING, 2, LINE * COUNT, LANES), f32),
            pltpu.VMEM((RING * LINE, COUNT, size), f32),
            pltpu.VMEM((RING * LINE, COUNT, size), f32),
            pltpu.VMEM((LINE * COUNT, size), f32),
            dma((COUNT + 2,)),
            dma((len(CHUNKS),)), dma((len(CHUNKS),)), dma, dma,
            dma((len(CHUNKS), 2)), dma((len(CHUNKS), 2)), dma((2,)), dma((2,)), dma((2,)), dma((2,)),
            dma((RING,)), dma((RING,)), dma, dma,
            dma((len(CHUNKS),)),
        ],
        compiler_params=pltpu.CompilerParams(collective_id=0, has_side_effects=True),
        name="schur",
    )(constraint_mats, primal_matrix, inverse_dual_iterate)


def solution(mesh):
    in_specs = (P(("narrow", "wide"), None, None), P(), P())
    out_specs = P(("narrow", "wide"), None)
    return jax.shard_map(body, mesh=mesh, in_specs=in_specs, out_specs=out_specs, check_vma=False)
```

```python
import jax
import jax.numpy as jnp
from jax import lax
from jax.experimental import pallas as pl
from jax.experimental.pallas import tpu as pltpu
from jax.sharding import PartitionSpec as P

PARTS = 16
LINE = 4
COUNT = 4
ROWS = 16
LANES = 128
RING = 8
DEPTH = ROWS * LANES
GROUP = PARTS * COUNT
FAR_FIRST = (4, 3, 5, 2, 6, 1, 7, 0)
CHUNKS = tuple((c, start, start + 8) for c in range(COUNT) for start in (0, 8))
DIAG_CHUNK = len(CHUNKS) - 2


def dot(a, b):
    return lax.dot_general(a, b, (((1,), (0,)), ((), ())), preferred_element_type=jnp.float32)


def dot_nt(a, b):
    return lax.dot_general(a, b, (((1,), (1,)), ((), ())), preferred_element_type=jnp.float32)


def pick_lanes(value, pick):
    high = value.astype(jnp.bfloat16)
    rest = value - high.astype(jnp.float32)
    mid = rest.astype(jnp.bfloat16)
    low = (rest - mid.astype(jnp.float32)).astype(jnp.bfloat16)
    return dot(high, pick) + dot(mid, pick) + dot(low, pick)


def kernel(a_hbm, x_hbm, z_hbm, out_ref, mats, primal_ref, dual_ref, send1, recv1, send1_diag, recv1_diag, wide_rows,
           diag_rows, v_all, a_all, v_diag, a_diag, partial, halves, sibling, send3, recv3, joined,
           load, s1, r1, s1d, r1d, s2, r2, s2d, r2d, sh, rh, s3, r3, own_sem):
    wide, narrow = lax.axis_index("wide"), lax.axis_index("narrow")
    z_hi = lax.div(narrow, 2)
    core = narrow - 2 * z_hi
    z_lo = lax.div(wide, 16)
    plane = wide - 16 * z_lo
    x = lax.div(plane, 4)
    y = plane - 4 * x
    z = z_hi * 4 + z_lo
    part = narrow * 4 + z_lo

    def wrap(value, size):
        return jnp.where(value >= size, value - size, value)

    column, same_core = [], []
    for dz in FAR_FIRST:
        z_at = wrap(z + dz, RING)
        hi = jnp.where(z_at >= 4, 1, 0)
        lo = z_at - 4 * hi
        for other in (0, 1):
            narrow_at = 2 * hi + (1 - core if other else core)
            if dz or other:
                column.append((narrow_at * 4 + lo, {"wide": lo * 16 + plane, "narrow": narrow_at}))
        same_core.append((z_at, lo * 16 + x * 4, 2 * hi + core))
    line_x, line_y = [], []
    for k in (2, 1, 3):
        x_at, y_at = wrap(x + k, LINE), wrap(y + k, LINE)
        line_x.append((x_at, {"wide": z_lo * 16 + x_at * 4 + y, "narrow": narrow}))
        line_y.append((y_at, {"wide": wide - y + y_at, "narrow": narrow}))
    sibling_core = {"wide": wide, "narrow": 2 * z_hi + 1 - core}

    barrier = pltpu.get_barrier_semaphore()
    greeted = [peer for _, peer in column + line_x + line_y]
    for peer in greeted:
        pl.semaphore_signal(barrier, inc=1, device_id=peer)

    loads = [pltpu.make_async_copy(x_hbm, primal_ref, load.at[4]), pltpu.make_async_copy(z_hbm, dual_ref, load.at[5])]
    for c in range(COUNT):
        loads.append(pltpu.make_async_copy(a_hbm.at[c], mats.at[c], load.at[c]))
    for copy in loads:
        copy.start()

    def remote(src, dst, send_sem, recv_sem, peer):
        return pltpu.make_async_remote_copy(
            src_ref=src, dst_ref=dst, send_sem=send_sem, recv_sem=recv_sem, device_id=peer
        )

    def wait_bytes(like, sem):
        pltpu.make_async_copy(like, like, sem).wait()

    def rows_of(k):
        c, start, stop = CHUNKS[k]
        return c, slice(2 * start, 2 * stop)

    def own1(k):
        c, rows = rows_of(k)
        return pltpu.make_async_copy(send1.at[c, part, rows], recv1.at[c, part, rows], own_sem.at[k])

    row = lax.broadcasted_iota(jnp.int32, (LANES, LANES), 0)
    col = lax.broadcasted_iota(jnp.int32, (LANES, LANES), 1)
    loads[0].wait()
    loads[1].wait()
    primal, dual = primal_ref[...], dual_ref[...]
    diag_a, diag_v = [], []
    for c in range(COUNT):
        loads[2 + c].wait()
        mat = mats[c]
        left = dot(primal, mat).astype(jnp.bfloat16)
        top = dot(left[:LANES], dual) + dot_nt(dual[:LANES], left)
        low = dot(left[LANES:], dual[:, LANES:]) + dot_nt(dual[LANES:], left[LANES:])
        mat32 = mat.astype(jnp.float32)
        a_up, a_low = mat32[:LANES, :LANES], mat32[LANES:, LANES:]
        fold_a = [mat[:LANES, LANES:], jnp.where(row <= col, a_up, a_low).astype(jnp.bfloat16)]
        corner = jnp.where(row < col, top[:, :LANES], jnp.where(row == col, 0.5 * top[:, :LANES], low))
        fold_v = [top[:, LANES:].astype(jnp.bfloat16), corner.astype(jnp.bfloat16)]
        diag_a.append(jnp.sum(jnp.where(row == col, a_low, 0.0), axis=0, keepdims=True))
        diag_v.append(jnp.sum(jnp.where(row == col, low, 0.0), axis=0, keepdims=True) * (0.5 / PARTS))
        for d in range(PARTS):
            half, at = d // 8, (d % 8) * ROWS
            for _, start, stop in [chunk for chunk in CHUNKS if chunk[0] == c]:
                send1[c, d, 2 * start:start + stop, :] = fold_a[half][at + start:at + stop]
                send1[c, d, start + stop:2 * stop, :] = fold_v[half][at + start:at + stop]
        if c == 0:
            pl.semaphore_wait(barrier, len(greeted))
        if c == COUNT - 1:
            send1_diag[...] = jnp.concatenate(diag_a + diag_v, axis=0).astype(jnp.bfloat16)
            for _, peer in column:
                remote(send1_diag, recv1_diag.at[part], s1d, r1d, peer).start()
        for k, chunk in enumerate(CHUNKS):
            if chunk[0] == c:
                _, rows = rows_of(k)
                for to, peer in column:
                    remote(send1.at[c, to, rows], recv1.at[c, part, rows], s1.at[k], r1.at[k], peer).start()
                own1(k).start()
    recv1_diag[part] = send1_diag[...]

    axes = ((v_all, v_diag, y, line_y), (a_all, a_diag, x, line_x))

    def lanes_of(k):
        _, start, stop = CHUNKS[k]
        return slice(start * LANES, stop * LANES)

    def send_lines(k):
        for axis, (ref, _, me, line) in enumerate(axes):
            at = ref.at[me, CHUNKS[k][0], :, lanes_of(k)]
            for _, peer in line:
                remote(at, at, s2.at[axis], r2.at[axis], peer).start()

    for k, (c, start, stop) in enumerate(CHUNKS):
        if k == DIAG_CHUNK:
            wait_bytes(recv1_diag.at[:PARTS - 1], r1d)
            for s in range(PARTS):
                diag_rows[pl.ds(RING * s, RING), :] = recv1_diag[s].astype(jnp.float32)
            for i in range(COUNT):
                at = slice(PARTS * i, PARTS * (i + 1))
                a_diag[x, at, :] = diag_rows[pl.ds(i, PARTS, stride=RING), :].astype(jnp.bfloat16)
                v_diag[y, at, :] = diag_rows[pl.ds(COUNT + i, PARTS, stride=RING), :].astype(jnp.bfloat16)
            for axis, (_, ref, me, line) in enumerate(axes):
                for _, peer in line:
                    remote(ref.at[me], ref.at[me], s2d.at[axis], r2d.at[axis], peer).start()
        size = stop - start
        own1(k).wait()
        wait_bytes(recv1.at[c, :PARTS - 1, rows_of(k)[1]], r1.at[k])
        for s in range(PARTS):
            block = recv1[c, s, 2 * start:2 * stop, :].astype(jnp.float32)
            wide_rows[k, 0, size * s:size * (s + 1), :] = block[:size]
            wide_rows[k, 1, size * s:size * (s + 1), :] = block[size:]
        for r in range(size):
            at = pl.ds((start + r) * LANES, LANES)
            a_all[x, c, :, at] = wide_rows[k, 0, pl.ds(r, PARTS, stride=size), :].astype(jnp.bfloat16)
            v_all[y, c, :, at] = wide_rows[k, 1, pl.ds(r, PARTS, stride=size), :].astype(jnp.bfloat16)
        send_lines(k)
    for axis, (ref, ref_diag, _, _) in enumerate(axes):
        wait_bytes(ref_diag.at[:LINE - 1], r2d.at[axis])
        wait_bytes(ref.at[:LINE - 1], r2.at[axis])

    size = LINE * GROUP
    v_mat, v_end = v_all[...].reshape(size, DEPTH), v_diag[...].reshape(size, LANES)
    product = dot_nt(v_mat, a_all[...].reshape(size, DEPTH)) + dot_nt(v_end, a_diag[...].reshape(size, LANES))
    for h in range(2):
        partial[h] = product[:, LANES * h:LANES * (h + 1)]

    def rows_for(owner, h):
        return partial[h, pl.ds(owner, LINE * COUNT, stride=PARTS), :]

    swaps = []
    for i, (z_at, base, narrow_at) in enumerate(same_core):
        lo = jnp.where(z_at >= 4, z_at - 4, z_at)
        for h in range(2):
            halves[i, h] = rows_for((narrow_at + 1 - 2 * core) * 4 + lo, h)
        swaps.append(remote(halves.at[i], sibling.at[i], sh.at[i], rh.at[i], sibling_core))
        swaps[i].start()
    own = z * LINE + y
    for i, (z_at, base, narrow_at) in enumerate(same_core):
        lo = jnp.where(z_at >= 4, z_at - 4, z_at)
        swaps[i].wait_recv()
        for h in range(2):
            both = rows_for(narrow_at * 4 + lo, h) + sibling[i, h]
            for k in range(LINE):
                send3[z_at * LINE + k, :, LANES * h:LANES * (h + 1)] = both[COUNT * k:COUNT * (k + 1)]
        for y_at, _ in line_y:
            peer = {"wide": base + y_at, "narrow": narrow_at}
            remote(send3.at[z_at * LINE + y_at], recv3.at[own], s3, r3, peer).start()
        if i < RING - 1:
            peer = {"wide": base + y, "narrow": narrow_at}
            remote(send3.at[z_at * LINE + y], recv3.at[own], s3, r3, peer).start()
    recv3[own] = send3[own]

    lane_from = lax.broadcasted_iota(jnp.int32, (size, size), 0)
    lane_to = lax.broadcasted_iota(jnp.int32, (size, size), 1)
    digit = lambda place: lax.rem(lax.div(lane_to, place), 4)
    first = digit(16) * 64 + digit(1) * 16 + digit(64) * 4 + digit(4)
    second = digit(4) * 64 + digit(16) * 16 + digit(64) * 4 + digit(1)
    pick1 = jnp.where(lane_from == first, 1.0, 0.0).astype(jnp.bfloat16)
    pick2 = jnp.where(lane_from == second, 1.0, 0.0).astype(jnp.bfloat16)

    wait_bytes(recv3.at[:RING * LINE - 1], r3)
    rows = []
    for k in range(LINE):
        total = recv3[k]
        for z_from in range(1, RING):
            total = total + recv3[z_from * LINE + k]
        rows.append(total)
    grouped = pick_lanes(jnp.concatenate(rows, axis=0), pick1)
    for k in range(LINE):
        for n in range(LINE):
            joined[COUNT * n:COUNT * (n + 1), GROUP * k:GROUP * (k + 1)] = grouped[
                COUNT * k:COUNT * (k + 1), GROUP * n:GROUP * (n + 1)
            ]
    ordered = pick_lanes(joined[...], pick2)
    for n in range(LINE):
        out_ref[:, size * n:size * (n + 1)] = ordered[COUNT * n:COUNT * (n + 1)]

    for k, (c, _, _) in enumerate(CHUNKS):
        wait_bytes(recv1.at[c, :PARTS - 1, rows_of(k)[1]], s1.at[k])
    wait_bytes(recv1_diag.at[:PARTS - 1], s1d)
    for axis in range(2):
        wait_bytes(v_all.at[:LINE - 1], s2.at[axis])
        wait_bytes(v_diag.at[:LINE - 1], s2d.at[axis])
    for swap in swaps:
        swap.wait_send()
    wait_bytes(recv3.at[:RING * LINE - 1], s3)


def body(constraint_mats, primal_matrix, inverse_dual_iterate):
    hbm = pl.BlockSpec(memory_space=pltpu.HBM)
    dma = pltpu.SemaphoreType.DMA
    bf16, f32 = jnp.bfloat16, jnp.float32
    order = 2 * LANES
    size = LINE * GROUP
    return pl.pallas_call(
        kernel,
        out_shape=jax.ShapeDtypeStruct((COUNT, 1024), f32),
        in_specs=[hbm] * 3,
        out_specs=pl.BlockSpec(memory_space=pltpu.VMEM),
        scratch_shapes=[
            pltpu.VMEM((COUNT, order, order), bf16),
            pltpu.VMEM((order, order), bf16),
            pltpu.VMEM((order, order), bf16),
            pltpu.VMEM((COUNT, PARTS, 2 * ROWS, LANES), bf16),
            pltpu.VMEM((COUNT, PARTS, 2 * ROWS, LANES), bf16),
            pltpu.VMEM((2 * COUNT, LANES), bf16),
            pltpu.VMEM((PARTS, 2 * COUNT, LANES), bf16),
            pltpu.VMEM((len(CHUNKS), 2, PARTS * ROWS // 2, LANES), f32),
            pltpu.VMEM((PARTS * 2 * COUNT, LANES), f32),
            pltpu.VMEM((LINE, COUNT, PARTS, DEPTH), bf16),
            pltpu.VMEM((LINE, COUNT, PARTS, DEPTH), bf16),
            pltpu.VMEM((LINE, GROUP, LANES), bf16),
            pltpu.VMEM((LINE, GROUP, LANES), bf16),
            pltpu.VMEM((2, size, LANES), f32),
            pltpu.VMEM((RING, 2, LINE * COUNT, LANES), f32),
            pltpu.VMEM((RING, 2, LINE * COUNT, LANES), f32),
            pltpu.VMEM((RING * LINE, COUNT, size), f32),
            pltpu.VMEM((RING * LINE, COUNT, size), f32),
            pltpu.VMEM((LINE * COUNT, size), f32),
            dma((COUNT + 2,)),
            dma((len(CHUNKS),)), dma((len(CHUNKS),)), dma, dma,
            dma((2,)), dma((2,)), dma((2,)), dma((2,)),
            dma((RING,)), dma((RING,)), dma, dma,
            dma((len(CHUNKS),)),
        ],
        compiler_params=pltpu.CompilerParams(collective_id=0, has_side_effects=True, vmem_limit_bytes=32 << 20),
        name="schur",
    )(*(pltpu.with_memory_space_constraint(m, pltpu.HBM) for m in (constraint_mats, primal_matrix, inverse_dual_iterate)))


def solution(mesh):
    in_specs = (P(("narrow", "wide"), None, None), P(), P())
    out_specs = P(("narrow", "wide"), None)
    return jax.shard_map(body, mesh=mesh, in_specs=in_specs, out_specs=out_specs, check_vma=False)
```

```python
import jax
import jax.numpy as jnp
from jax import lax
from jax.experimental import pallas as pl
from jax.experimental.pallas import tpu as pltpu
from jax.sharding import PartitionSpec as P

RING = 8
LINE = 4
COUNT = 4
LANES = 128
ROWS = 32
UNIT = 8
DEPTH = ROWS * LANES
FAR_FIRST = (4, 3, 5, 2, 6, 1, 7, 0)
UNITS = tuple((pair, quarter) for pair in range(2) for quarter in range(4))
LAST = len(UNITS) - 1
ORDER = [("a", 0), ("a", 1)] + [w for u in range(LAST - 1) for w in (("v", u), ("a", u + 2))] + [("v", LAST - 1), ("v", LAST)]
SLOT = {what: 16 * i for i, what in enumerate(ORDER)}
MESSAGES = tuple([(0, 3)] + [(2 * k + 1, 2 * k + 3) for k in range(1, LAST)] + [(2 * LAST + 1, 2 * LAST + 2)])
DIAG_MESSAGE = 4


def dot(a, b):
    return lax.dot_general(a, b, (((1,), (0,)), ((), ())), preferred_element_type=jnp.float32)


def dot_nt(a, b):
    return lax.dot_general(a, b, (((1,), (1,)), ((), ())), preferred_element_type=jnp.float32)


def pick_lanes(value, pick):
    high = value.astype(jnp.bfloat16)
    rest = value - high.astype(jnp.float32)
    mid = rest.astype(jnp.bfloat16)
    low = (rest - mid.astype(jnp.float32)).astype(jnp.bfloat16)
    return dot(high, pick) + dot(mid, pick) + dot(low, pick)


def kernel(a_hbm, x_hbm, z_hbm, out_ref, mats, primal_ref, dual_ref, send1, recv1, send1_diag, recv1_diag, wide_rows,
           diag_rows, v_all, a_all, v_diag, a_diag, partial, send3, recv3, joined,
           load, s1, r1, s1d, r1d, s2, r2v, r2a, s2d, r2d, sc, rc, s3, r3, own_sem):
    wide, narrow = lax.axis_index("wide"), lax.axis_index("narrow")
    z_hi = lax.div(narrow, 2)
    core = narrow - 2 * z_hi
    z_lo = lax.div(wide, 16)
    plane = wide - 16 * z_lo
    x = lax.div(plane, 4)
    y = plane - 4 * x
    z = z_hi * 4 + z_lo

    def wrap(value, size):
        return jnp.where(value >= size, value - size, value)

    column, same_core = [], []
    for dz in FAR_FIRST:
        z_at = wrap(z + dz, RING)
        hi = jnp.where(z_at >= 4, 1, 0)
        lo = z_at - 4 * hi
        if dz:
            column.append((z_at, {"wide": lo * 16 + plane, "narrow": 2 * hi + core}))
        same_core.append((z_at, lo * 16 + x * 4, 2 * hi + core))
    line_x, line_y = [], []
    for k in (2, 1, 3):
        x_at, y_at = wrap(x + k, LINE), wrap(y + k, LINE)
        line_x.append((x_at, {"wide": z_lo * 16 + x_at * 4 + y, "narrow": narrow}))
        line_y.append((y_at, {"wide": wide - y + y_at, "narrow": narrow}))
    sibling_core = {"wide": wide, "narrow": 2 * z_hi + 1 - core}

    barrier = pltpu.get_barrier_semaphore()
    greeted = [peer for _, peer in column + line_x + line_y] + [sibling_core]
    for peer in greeted:
        pl.semaphore_signal(barrier, inc=1, device_id=peer)

    loads = [pltpu.make_async_copy(x_hbm, primal_ref, load.at[4]), pltpu.make_async_copy(z_hbm, dual_ref, load.at[5])]
    for c in range(COUNT):
        loads.append(pltpu.make_async_copy(a_hbm.at[c], mats.at[c], load.at[c]))
    for copy in loads:
        copy.start()

    def remote(src, dst, send_sem, recv_sem, peer):
        return pltpu.make_async_remote_copy(
            src_ref=src, dst_ref=dst, send_sem=send_sem, recv_sem=recv_sem, device_id=peer
        )

    def wait_bytes(like, sem):
        pltpu.make_async_copy(like, like, sem).wait()

    def rows_of(k):
        first, end = MESSAGES[k]
        return slice(16 * first, 16 * end)

    def own1(k):
        return pltpu.make_async_copy(send1.at[z, rows_of(k)], recv1.at[z, rows_of(k)], own_sem.at[k])

    def send_column(k):
        for to, peer in column:
            remote(send1.at[to, rows_of(k)], recv1.at[z, rows_of(k)], s1.at[k], r1.at[k], peer).start()
        own1(k).start()

    def store_units(kind, c, fold):
        for d in range(RING):
            for quarter in range(4):
                at = d % 4 * ROWS + quarter * UNIT
                slot = SLOT[kind, c // 2 * 4 + quarter] + c % 2 * UNIT
                send1[d, slot:slot + UNIT, :] = fold[d // 4][at:at + UNIT]

    row = lax.broadcasted_iota(jnp.int32, (LANES, LANES), 0)
    col = lax.broadcasted_iota(jnp.int32, (LANES, LANES), 1)
    loads[0].wait()
    loads[1].wait()
    primal, dual = primal_ref[...], dual_ref[...]
    diag_a, diag_v = [], []
    for c in range(COUNT):
        loads[2 + c].wait()
        mat = mats[c]
        mat32 = mat.astype(jnp.float32)
        a_up, a_low = mat32[:LANES, :LANES], mat32[LANES:, LANES:]
        store_units("a", c, [mat[:LANES, LANES:], jnp.where(row <= col, a_up, a_low).astype(jnp.bfloat16)])
        diag_a.append(jnp.sum(jnp.where(row == col, a_low, 0.0), axis=0, keepdims=True))
    for c in range(COUNT):
        mat = mats[c]
        left = dot(primal, mat).astype(jnp.bfloat16)
        top = dot(left[:LANES], dual) + dot_nt(dual[:LANES], left)
        low = dot(left[LANES:], dual[:, LANES:]) + dot_nt(dual[LANES:], left[LANES:])
        corner = jnp.where(row < col, top[:, :LANES], jnp.where(row == col, 0.5 * top[:, :LANES], low))
        store_units("v", c, [top[:, LANES:].astype(jnp.bfloat16), corner.astype(jnp.bfloat16)])
        diag_v.append(jnp.sum(jnp.where(row == col, low, 0.0), axis=0, keepdims=True) * (0.5 / RING))
        if c == 1:
            pl.semaphore_wait(barrier, len(greeted))
            for k in range(DIAG_MESSAGE):
                send_column(k)
    send1_diag[...] = jnp.concatenate(diag_a + diag_v, axis=0).astype(jnp.bfloat16)
    for _, peer in column:
        remote(send1_diag, recv1_diag.at[z], s1d, r1d, peer).start()
    for k in range(DIAG_MESSAGE, len(MESSAGES)):
        send_column(k)
    recv1_diag[z] = send1_diag[...]

    def block(kind, u, who):
        pair, quarter = UNITS[u]
        lanes = slice(quarter * UNIT * LANES, (quarter + 1) * UNIT * LANES)
        return v_all.at[who, pair, :, lanes] if kind == "v" else a_all.at[core, who, pair, :, lanes]

    def pass_on(u):
        wait_bytes(block("a", u, slice(0, LINE - 1)), r2a.at[u])
        whole = block("a", u, slice(None))
        remote(whole, whole, sc, rc, sibling_core).start()

    for k, (first, end) in enumerate(MESSAGES):
        own1(k).wait()
        wait_bytes(recv1.at[:RING - 1, rows_of(k)], r1.at[k])
        for kind, u in ORDER[first:end]:
            slot = SLOT[kind, u]
            for s in range(RING):
                wide_rows[slot // 16, 16 * s:16 * (s + 1), :] = recv1[s, slot:slot + 16, :].astype(jnp.float32)
            to = block(kind, u, y if kind == "v" else x)
            for r in range(UNIT):
                both = [wide_rows[slot // 16, pl.ds(half * UNIT + r, RING, stride=16), :] for half in range(2)]
                to[:, r * LANES:(r + 1) * LANES] = jnp.concatenate(both, axis=0).astype(jnp.bfloat16)
            for _, peer in (line_y if kind == "v" else line_x):
                remote(to, to, s2.at[0 if kind == "v" else 1], r2v if kind == "v" else r2a.at[u], peer).start()
        if k == DIAG_MESSAGE:
            wait_bytes(recv1_diag.at[:RING - 1], r1d)
            for s in range(RING):
                diag_rows[pl.ds(2 * COUNT * s, 2 * COUNT), :] = recv1_diag[s].astype(jnp.float32)
            ends = [diag_rows[pl.ds(i, RING, stride=2 * COUNT), :] for i in range(2 * COUNT)]
            a_diag[core, x] = jnp.concatenate(ends[:COUNT], axis=0).astype(jnp.bfloat16)
            v_diag[y] = jnp.concatenate(ends[COUNT:], axis=0).astype(jnp.bfloat16)
            for axis, (at, line) in enumerate(((v_diag.at[y], line_y), (a_diag.at[core, x], line_x))):
                for _, peer in line:
                    remote(at, at, s2d.at[axis], r2d.at[axis], peer).start()
        if k >= 2:
            pass_on(k - 2)
    wait_bytes(a_diag.at[0, :LINE - 1], r2d.at[1])
    remote(a_diag.at[core], a_diag.at[core], s2d.at[2], r2d.at[2], sibling_core).start()
    pass_on(LAST - 1)
    pass_on(LAST)
    wait_bytes(v_diag.at[:LINE - 1], r2d.at[0])
    wait_bytes(v_all.at[:LINE - 1], r2v)
    wait_bytes(a_diag.at[0], r2d.at[2])
    wait_bytes(a_all.at[0], rc)

    rows, size = LINE * COUNT * RING, 2 * LINE * COUNT * RING
    product = dot_nt(v_all[...].reshape(rows, DEPTH), a_all[...].reshape(size, DEPTH)) + dot_nt(
        v_diag[...].reshape(rows, LANES), a_diag[...].reshape(size, LANES)
    )
    for h in range(2):
        partial[h] = product[:, LANES * h:LANES * (h + 1)]
    own = z * LINE + y
    for i, (z_at, base, narrow_at) in enumerate(same_core):
        for h in range(2):
            piece = partial[h, pl.ds(z_at, LINE * COUNT, stride=RING), :]
            for k in range(LINE):
                send3[z_at * LINE + k, :, LANES * h:LANES * (h + 1)] = piece[COUNT * k:COUNT * (k + 1)]
        for y_at in [y_at for y_at, _ in line_y] + ([y] if i < RING - 1 else []):
            peer = {"wide": base + y_at, "narrow": narrow_at}
            remote(send3.at[z_at * LINE + y_at], recv3.at[own], s3, r3, peer).start()
    recv3[own] = send3[own]

    lane_from = lax.broadcasted_iota(jnp.int32, (size, size), 0)
    lane_to = lax.broadcasted_iota(jnp.int32, (size, size), 1)
    digit = lambda place: lax.rem(lax.div(lane_to, place), 4)
    odd = lax.rem(digit(64), 2)
    first = odd * 128 + digit(16) * 32 + digit(1) * 8 + lax.div(digit(64), 2) * 4 + digit(4)
    second = digit(4) * 64 + digit(16) * 16 + digit(64) * 4 + digit(1)
    pick1 = jnp.where(lane_from == first, 1.0, 0.0).astype(jnp.bfloat16)
    pick2 = jnp.where(lane_from == second, 1.0, 0.0).astype(jnp.bfloat16)

    wait_bytes(recv3.at[:RING * LINE - 1], r3)
    totals = []
    for k in range(LINE):
        total = recv3[k]
        for z_from in range(1, RING):
            total = total + recv3[z_from * LINE + k]
        totals.append(total)
    grouped = pick_lanes(jnp.concatenate(totals, axis=0), pick1)
    for k in range(LINE):
        for n in range(LINE):
            joined[COUNT * n:COUNT * (n + 1), 64 * k:64 * (k + 1)] = grouped[
                COUNT * k:COUNT * (k + 1), 64 * n:64 * (n + 1)
            ]
    ordered = pick_lanes(joined[...], pick2)
    for n in range(LINE):
        out_ref[:, size * n:size * (n + 1)] = ordered[COUNT * n:COUNT * (n + 1)]

    for k in range(len(MESSAGES)):
        wait_bytes(recv1.at[:RING - 1, rows_of(k)], s1.at[k])
    wait_bytes(recv1_diag.at[:RING - 1], s1d)
    wait_bytes(v_all.at[:LINE - 1], s2.at[0])
    wait_bytes(a_all.at[0, :LINE - 1], s2.at[1])
    wait_bytes(v_diag.at[:LINE - 1], s2d.at[0])
    wait_bytes(a_diag.at[0, :LINE - 1], s2d.at[1])
    wait_bytes(a_diag.at[0], s2d.at[2])
    wait_bytes(a_all.at[0], sc)
    wait_bytes(recv3.at[:RING * LINE - 1], s3)


def body(constraint_mats, primal_matrix, inverse_dual_iterate):
    hbm = pl.BlockSpec(memory_space=pltpu.HBM)
    dma = pltpu.SemaphoreType.DMA
    bf16, f32 = jnp.bfloat16, jnp.float32
    order = 2 * LANES
    rows, size = LINE * COUNT * RING, 2 * LINE * COUNT * RING
    return pl.pallas_call(
        kernel,
        out_shape=jax.ShapeDtypeStruct((COUNT, 1024), f32),
        in_specs=[hbm] * 3,
        out_specs=pl.BlockSpec(memory_space=pltpu.VMEM),
        scratch_shapes=[
            pltpu.VMEM((COUNT, order, order), bf16),
            pltpu.VMEM((order, order), bf16),
            pltpu.VMEM((order, order), bf16),
            pltpu.VMEM((RING, 16 * len(ORDER), LANES), bf16),
            pltpu.VMEM((RING, 16 * len(ORDER), LANES), bf16),
            pltpu.VMEM((2 * COUNT, LANES), bf16),
            pltpu.VMEM((RING, 2 * COUNT, LANES), bf16),
            pltpu.VMEM((len(ORDER), RING * 16, LANES), f32),
            pltpu.VMEM((RING * 2 * COUNT, LANES), f32),
            pltpu.VMEM((LINE, 2, 16, DEPTH), bf16),
            pltpu.VMEM((2, LINE, 2, 16, DEPTH), bf16),
            pltpu.VMEM((LINE, COUNT * RING, LANES), bf16),
            pltpu.VMEM((2, LINE, COUNT * RING, LANES), bf16),
            pltpu.VMEM((2, rows, LANES), f32),
            pltpu.VMEM((RING * LINE, COUNT, size), f32),
            pltpu.VMEM((RING * LINE, COUNT, size), f32),
            pltpu.VMEM((LINE * COUNT, size), f32),
            dma((COUNT + 2,)),
            dma((len(MESSAGES),)), dma((len(MESSAGES),)), dma, dma,
            dma((2,)), dma, dma((len(UNITS),)), dma((3,)), dma((3,)), dma, dma,
            dma, dma,
            dma((len(MESSAGES),)),
        ],
        compiler_params=pltpu.CompilerParams(collective_id=0, has_side_effects=True, vmem_limit_bytes=32 << 20),
        name="schur",
    )(*(pltpu.with_memory_space_constraint(m, pltpu.HBM) for m in (constraint_mats, primal_matrix, inverse_dual_iterate)))


def solution(mesh):
    in_specs = (P(("narrow", "wide"), None, None), P(), P())
    out_specs = P(("narrow", "wide"), None)
    return jax.shard_map(body, mesh=mesh, in_specs=in_specs, out_specs=out_specs, check_vma=False)
```

```python
import jax
import jax.numpy as jnp
from jax import lax
from jax.experimental import pallas as pl
from jax.experimental.pallas import tpu as pltpu
from jax.sharding import PartitionSpec as P

RING = 8
LINE = 4
COUNT = 4
LANES = 128
ROWS = 32
UNIT = 8
DEPTH = ROWS * LANES
FAR_FIRST = (4, 3, 5, 2, 6, 1, 7, 0)
UNITS = tuple((pair, quarter) for pair in range(2) for quarter in range(4))
LAST = len(UNITS) - 1
ORDER = [("a", 0), ("a", 1)] + [w for u in range(LAST - 1) for w in (("v", u), ("a", u + 2))] + [("v", LAST - 1), ("v", LAST)]
SLOT = {what: 16 * i for i, what in enumerate(ORDER)}
MESSAGES = tuple([(0, 2), (2, 3)] + [(2 * k + 1, 2 * k + 3) for k in range(1, LAST)] + [(2 * LAST + 1, 2 * LAST + 2)])
DIAG_MESSAGE = 5


def dot(a, b):
    return lax.dot_general(a, b, (((1,), (0,)), ((), ())), preferred_element_type=jnp.float32)


def dot_nt(a, b):
    return lax.dot_general(a, b, (((1,), (1,)), ((), ())), preferred_element_type=jnp.float32)


def pick_lanes(value, pick):
    high = value.astype(jnp.bfloat16)
    rest = value - high.astype(jnp.float32)
    mid = rest.astype(jnp.bfloat16)
    low = (rest - mid.astype(jnp.float32)).astype(jnp.bfloat16)
    count = value.shape[0]
    parts = dot(jnp.concatenate([high, mid, low], axis=0), pick)
    return parts[:count] + parts[count:2 * count] + parts[2 * count:]


def kernel(a_hbm, x_hbm, z_hbm, out_ref, mats, primal_ref, dual_ref, send1, recv1, send1_diag, recv1_diag, wide_rows,
           diag_rows, v_all, a_all, v_diag, a_diag, partial, send3, recv3,
           load, s1, r1, s1d, r1d, s2, r2v, r2a, s2d, r2d, sc, rc, s3, r3, own_sem):
    wide, narrow = lax.axis_index("wide"), lax.axis_index("narrow")
    z_hi = lax.div(narrow, 2)
    core = narrow - 2 * z_hi
    z_lo = lax.div(wide, 16)
    plane = wide - 16 * z_lo
    x = lax.div(plane, 4)
    y = plane - 4 * x
    z = z_hi * 4 + z_lo

    def wrap(value, size):
        return jnp.where(value >= size, value - size, value)

    column, same_core = [], []
    for dz in FAR_FIRST:
        z_at = wrap(z + dz, RING)
        hi = jnp.where(z_at >= 4, 1, 0)
        lo = z_at - 4 * hi
        if dz:
            column.append((z_at, {"wide": lo * 16 + plane, "narrow": 2 * hi + core}))
        same_core.append((z_at, lo * 16 + x * 4, 2 * hi + core))
    line_x, line_y = [], []
    for k in (2, 1, 3):
        x_at, y_at = wrap(x + k, LINE), wrap(y + k, LINE)
        line_x.append((x_at, {"wide": z_lo * 16 + x_at * 4 + y, "narrow": narrow}))
        line_y.append((y_at, {"wide": wide - y + y_at, "narrow": narrow}))
    sibling_core = {"wide": wide, "narrow": 2 * z_hi + 1 - core}

    barrier = pltpu.get_barrier_semaphore()
    greeted = [peer for _, peer in column + line_x + line_y] + [sibling_core]
    for peer in greeted:
        pl.semaphore_signal(barrier, inc=1, device_id=peer)

    loads = [pltpu.make_async_copy(x_hbm, primal_ref, load.at[4]), pltpu.make_async_copy(z_hbm, dual_ref, load.at[5])]
    for c in range(COUNT):
        loads.append(pltpu.make_async_copy(a_hbm.at[c], mats.at[c], load.at[c]))
    for i in (2, 3, 0, 1, 4, 5):
        loads[i].start()

    def remote(src, dst, send_sem, recv_sem, peer):
        return pltpu.make_async_remote_copy(
            src_ref=src, dst_ref=dst, send_sem=send_sem, recv_sem=recv_sem, device_id=peer
        )

    def wait_bytes(like, sem):
        pltpu.make_async_copy(like, like, sem).wait()

    def rows_of(k):
        first, end = MESSAGES[k]
        return slice(16 * first, 16 * end)

    def own1(k):
        return pltpu.make_async_copy(send1.at[z, rows_of(k)], recv1.at[z, rows_of(k)], own_sem.at[k])

    def send_column(k):
        for to, peer in column:
            remote(send1.at[to, rows_of(k)], recv1.at[z, rows_of(k)], s1.at[k], r1.at[k], peer).start()
        own1(k).start()

    def store_units(kind, c, fold):
        for d in range(RING):
            for quarter in range(4):
                at = d % 4 * ROWS + quarter * UNIT
                slot = SLOT[kind, c // 2 * 4 + quarter] + c % 2 * UNIT
                send1[d, slot:slot + UNIT, :] = fold[d // 4][at:at + UNIT]

    row = lax.broadcasted_iota(jnp.int32, (LANES, LANES), 0)
    col = lax.broadcasted_iota(jnp.int32, (LANES, LANES), 1)
    diag_a, diag_v = [], []
    for c in range(COUNT):
        loads[2 + c].wait()
        mat = mats[c]
        mat32 = mat.astype(jnp.float32)
        a_up, a_low = mat32[:LANES, :LANES], mat32[LANES:, LANES:]
        store_units("a", c, [mat[:LANES, LANES:], jnp.where(row <= col, a_up, a_low).astype(jnp.bfloat16)])
        diag_a.append(jnp.sum(jnp.where(row == col, a_low, 0.0), axis=0, keepdims=True))
        if c == 1:
            pl.semaphore_wait(barrier, len(greeted))
            send_column(0)
    loads[0].wait()
    loads[1].wait()
    primal, dual = primal_ref[...], dual_ref[...]
    for c in range(COUNT):
        mat = mats[c]
        left = dot(primal, mat).astype(jnp.bfloat16)
        top = dot(left[:LANES], dual) + dot_nt(dual[:LANES], left)
        low = dot(left[LANES:], dual[:, LANES:]) + dot_nt(dual[LANES:], left[LANES:])
        corner = jnp.where(row < col, top[:, :LANES], jnp.where(row == col, 0.5 * top[:, :LANES], low))
        store_units("v", c, [top[:, LANES:].astype(jnp.bfloat16), corner.astype(jnp.bfloat16)])
        diag_v.append(jnp.sum(jnp.where(row == col, low, 0.0), axis=0, keepdims=True) * (0.5 / RING))
        if c == 1:
            for k in range(1, DIAG_MESSAGE):
                send_column(k)
    send1_diag[...] = jnp.concatenate(diag_a + diag_v, axis=0).astype(jnp.bfloat16)
    for _, peer in column:
        remote(send1_diag, recv1_diag.at[z], s1d, r1d, peer).start()
    for k in range(DIAG_MESSAGE, len(MESSAGES)):
        send_column(k)
    recv1_diag[z] = send1_diag[...]

    def block(kind, u, who):
        pair, quarter = UNITS[u]
        lanes = slice(quarter * UNIT * LANES, (quarter + 1) * UNIT * LANES)
        return v_all.at[who, pair, :, lanes] if kind == "v" else a_all.at[core, who, pair, :, lanes]

    def pass_on(u):
        wait_bytes(block("a", u, slice(0, LINE - 1)), r2a.at[u])
        whole = block("a", u, slice(None))
        remote(whole, whole, sc, rc.at[u // LAST], sibling_core).start()

    for k, (first, end) in enumerate(MESSAGES):
        own1(k).wait()
        wait_bytes(recv1.at[:RING - 1, rows_of(k)], r1.at[k])
        for kind, u in ORDER[first:end]:
            slot = SLOT[kind, u]
            for s in range(RING):
                wide_rows[slot // 16, 16 * s:16 * (s + 1), :] = recv1[s, slot:slot + 16, :].astype(jnp.float32)
            to = block(kind, u, y if kind == "v" else x)
            for r in range(UNIT):
                both = [wide_rows[slot // 16, pl.ds(half * UNIT + r, RING, stride=16), :] for half in range(2)]
                to[:, r * LANES:(r + 1) * LANES] = jnp.concatenate(both, axis=0).astype(jnp.bfloat16)
            for _, peer in (line_y if kind == "v" else line_x):
                remote(to, to, s2.at[0 if kind == "v" else 1], r2v.at[u // LAST] if kind == "v" else r2a.at[u], peer).start()
        if k == DIAG_MESSAGE:
            wait_bytes(recv1_diag.at[:RING - 1], r1d)
            for s in range(RING):
                diag_rows[pl.ds(2 * COUNT * s, 2 * COUNT), :] = recv1_diag[s].astype(jnp.float32)
            ends = [diag_rows[pl.ds(i, RING, stride=2 * COUNT), :] for i in range(2 * COUNT)]
            a_diag[core, x] = jnp.concatenate(ends[:COUNT], axis=0).astype(jnp.bfloat16)
            v_diag[y] = jnp.concatenate(ends[COUNT:], axis=0).astype(jnp.bfloat16)
            for axis, (at, line) in enumerate(((v_diag.at[y], line_y), (a_diag.at[core, x], line_x))):
                for _, peer in line:
                    remote(at, at, s2d.at[axis], r2d.at[axis], peer).start()
        if k >= 3:
            pass_on(k - 3)
    wait_bytes(a_diag.at[0, :LINE - 1], r2d.at[1])
    remote(a_diag.at[core], a_diag.at[core], s2d.at[2], r2d.at[2], sibling_core).start()
    pass_on(LAST - 1)
    pass_on(LAST)

    rows, size = LINE * COUNT * RING, 2 * LINE * COUNT * RING
    wait_bytes(v_diag.at[:LINE - 1], r2d.at[0])
    wait_bytes(a_diag.at[0], r2d.at[2])
    product = dot_nt(v_diag[...].reshape(rows, LANES), a_diag[...].reshape(size, LANES))
    most = LAST % 4 * UNIT * LANES
    seven = DEPTH * LAST // len(UNITS)
    wait_bytes(v_all.at[:LINE - 1, :, :, :seven], r2v.at[0])
    wait_bytes(a_all.at[0, :, :, :, :seven], rc.at[0])
    product += dot_nt(v_all[:, :, :, :most].reshape(rows, most), a_all[:, :, :, :, :most].reshape(size, most))
    wait_bytes(v_all.at[:LINE - 1, 0, :, most:], r2v.at[1])
    wait_bytes(a_all.at[0, :, 0, :, most:], rc.at[1])
    product += dot_nt(v_all[:, :, :, most:].reshape(rows, DEPTH - most), a_all[:, :, :, :, most:].reshape(size, DEPTH - most))
    for h in range(2):
        partial[h] = product[:, LANES * h:LANES * (h + 1)]
    own = z * LINE + y
    for i, (z_at, base, narrow_at) in enumerate(same_core):
        for h in range(2):
            piece = partial[h, pl.ds(z_at, LINE * COUNT, stride=RING), :]
            for k in range(LINE):
                send3[z_at * LINE + k, :, LANES * h:LANES * (h + 1)] = piece[COUNT * k:COUNT * (k + 1)]
        for y_at in [y_at for y_at, _ in line_y] + ([y] if i < RING - 1 else []):
            peer = {"wide": base + y_at, "narrow": narrow_at}
            remote(send3.at[z_at * LINE + y_at], recv3.at[own], s3, r3, peer).start()
    recv3[own] = send3[own]

    lane_from = lax.broadcasted_iota(jnp.int32, (size, 4 * size), 0)
    lane_to = lax.broadcasted_iota(jnp.int32, (size, 4 * size), 1)
    digit = lambda place, base=4: lax.rem(lax.div(lane_to, place), base)
    source = digit(256, 2) * 128 + digit(16) * 32 + digit(1) * 8 + digit(512, 2) * 4 + digit(64)
    pick = jnp.where((lane_from == source) & (digit(4) == 0), 1.0, 0.0).astype(jnp.bfloat16)

    wait_bytes(recv3.at[:RING * LINE - 1], r3)
    totals = []
    for k in range(LINE):
        total = recv3[k]
        for z_from in range(1, RING):
            total = total + recv3[z_from * LINE + k]
        totals.append(total)
    ordered = pick_lanes(jnp.concatenate(totals, axis=0), pick)
    result = ordered[:COUNT]
    for k in range(1, LINE):
        result = result + pltpu.roll(ordered, COUNT * k, 1)[COUNT * k:COUNT * (k + 1)]
    out_ref[...] = result

    for k in range(len(MESSAGES)):
        wait_bytes(recv1.at[:RING - 1, rows_of(k)], s1.at[k])
    wait_bytes(recv1_diag.at[:RING - 1], s1d)
    wait_bytes(v_all.at[:LINE - 1], s2.at[0])
    wait_bytes(a_all.at[0, :LINE - 1], s2.at[1])
    wait_bytes(v_diag.at[:LINE - 1], s2d.at[0])
    wait_bytes(a_diag.at[0, :LINE - 1], s2d.at[1])
    wait_bytes(a_diag.at[0], s2d.at[2])
    wait_bytes(a_all.at[0], sc)
    wait_bytes(recv3.at[:RING * LINE - 1], s3)


def body(constraint_mats, primal_matrix, inverse_dual_iterate):
    hbm = pl.BlockSpec(memory_space=pltpu.HBM)
    dma = pltpu.SemaphoreType.DMA
    bf16, f32 = jnp.bfloat16, jnp.float32
    order = 2 * LANES
    rows, size = LINE * COUNT * RING, 2 * LINE * COUNT * RING
    return pl.pallas_call(
        kernel,
        out_shape=jax.ShapeDtypeStruct((COUNT, 1024), f32),
        in_specs=[hbm] * 3,
        out_specs=pl.BlockSpec(memory_space=pltpu.VMEM),
        scratch_shapes=[
            pltpu.VMEM((COUNT, order, order), bf16),
            pltpu.VMEM((order, order), bf16),
            pltpu.VMEM((order, order), bf16),
            pltpu.VMEM((RING, 16 * len(ORDER), LANES), bf16),
            pltpu.VMEM((RING, 16 * len(ORDER), LANES), bf16),
            pltpu.VMEM((2 * COUNT, LANES), bf16),
            pltpu.VMEM((RING, 2 * COUNT, LANES), bf16),
            pltpu.VMEM((len(ORDER), RING * 16, LANES), f32),
            pltpu.VMEM((RING * 2 * COUNT, LANES), f32),
            pltpu.VMEM((LINE, 2, 16, DEPTH), bf16),
            pltpu.VMEM((2, LINE, 2, 16, DEPTH), bf16),
            pltpu.VMEM((LINE, COUNT * RING, LANES), bf16),
            pltpu.VMEM((2, LINE, COUNT * RING, LANES), bf16),
            pltpu.VMEM((2, rows, LANES), f32),
            pltpu.VMEM((RING * LINE, COUNT, size), f32),
            pltpu.VMEM((RING * LINE, COUNT, size), f32),
            dma((COUNT + 2,)),
            dma((len(MESSAGES),)), dma((len(MESSAGES),)), dma, dma,
            dma((2,)), dma((2,)), dma((len(UNITS),)), dma((3,)), dma((3,)), dma, dma((2,)),
            dma, dma,
            dma((len(MESSAGES),)),
        ],
        compiler_params=pltpu.CompilerParams(collective_id=0, has_side_effects=True, vmem_limit_bytes=32 << 20),
        name="schur",
    )(*(pltpu.with_memory_space_constraint(m, pltpu.HBM) for m in (constraint_mats, primal_matrix, inverse_dual_iterate)))


def solution(mesh):
    in_specs = (P(("narrow", "wide"), None, None), P(), P())
    out_specs = P(("narrow", "wide"), None)
    return jax.shard_map(body, mesh=mesh, in_specs=in_specs, out_specs=out_specs, check_vma=False)
```

```python
import jax
import jax.numpy as jnp
from jax import lax
from jax.experimental import pallas as pl
from jax.experimental.pallas import tpu as pltpu
from jax.sharding import PartitionSpec as P

RING = 8
LINE = 4
COUNT = 4
LANES = 128
ROWS = 32
UNIT = 8
DEPTH = ROWS * LANES
FAR_FIRST = (4, 3, 5, 2, 6, 1, 7)
UNITS = tuple((pair, quarter) for pair in range(2) for quarter in range(4))
LAST = len(UNITS) - 1
ORDER = [("a", 0), ("a", 1), ("a", 2)] + [w for u in range(LAST - 2) for w in (("v", u), ("a", u + 3))] + [("v", LAST - 2), ("v", LAST - 1), ("v", LAST)]
SLOT = {what: 16 * i for i, what in enumerate(ORDER)}
MESSAGES = ((0, 2), (2, 4), (4, 6), (6, 8), (8, 10), (10, 12), (12, 14), (14, 15), (15, 16))
DIAG_MESSAGE = 5


def dot(a, b):
    return lax.dot_general(a, b, (((1,), (0,)), ((), ())), preferred_element_type=jnp.float32)


def dot_nt(a, b):
    return lax.dot_general(a, b, (((1,), (1,)), ((), ())), preferred_element_type=jnp.float32)


def pick_lanes(value, pick):
    high = value.astype(jnp.bfloat16)
    rest = value - high.astype(jnp.float32)
    mid = rest.astype(jnp.bfloat16)
    low = (rest - mid.astype(jnp.float32)).astype(jnp.bfloat16)
    count = value.shape[0]
    parts = dot(jnp.concatenate([high, mid, low], axis=0), pick)
    return parts[:count] + parts[count:2 * count] + parts[2 * count:]


def kernel(a_hbm, x_hbm, z_hbm, out_ref, mats, primal_ref, dual_ref, send1, recv1, send1_diag, recv1_diag, wide_rows,
           diag_rows, v_all, a_all, v_diag, a_diag, partial, send3, recv3,
           load, s1, r1, s1d, r1d, s2, r2v, r2a, s2d, r2d, sc, rc, s3, r3, own_sem):
    wide, narrow = lax.axis_index("wide"), lax.axis_index("narrow")
    z_hi = lax.div(narrow, 2)
    core = narrow - 2 * z_hi
    z_lo = lax.div(wide, 16)
    plane = wide - 16 * z_lo
    x = lax.div(plane, 4)
    y = plane - 4 * x
    z = z_hi * 4 + z_lo

    def wrap(value, size):
        return jnp.where(value >= size, value - size, value)

    column = []
    for dz in FAR_FIRST:
        z_at = wrap(z + dz, RING)
        hi = jnp.where(z_at >= 4, 1, 0)
        lo = z_at - 4 * hi
        column.append((z_at, {"wide": lo * 16 + plane, "narrow": 2 * hi + core}))
    line_x, line_y = [], []
    for k in (2, 1, 3):
        x_at, y_at = wrap(x + k, LINE), wrap(y + k, LINE)
        line_x.append((x_at, {"wide": z_lo * 16 + x_at * 4 + y, "narrow": narrow}))
        line_y.append((y_at, {"wide": wide - y + y_at, "narrow": narrow}))
    sibling_core = {"wide": wide, "narrow": 2 * z_hi + 1 - core}

    barrier = pltpu.get_barrier_semaphore()
    greeted = [peer for _, peer in column + line_x + line_y] + [sibling_core]
    for peer in greeted:
        pl.semaphore_signal(barrier, inc=1, device_id=peer)

    loads = [pltpu.make_async_copy(x_hbm, primal_ref, load.at[4]), pltpu.make_async_copy(z_hbm, dual_ref, load.at[5])]
    for c in range(COUNT):
        loads.append(pltpu.make_async_copy(a_hbm.at[c], mats.at[c], load.at[c]))
    for i in (2, 3, 0, 1, 4, 5):
        loads[i].start()

    def remote(src, dst, send_sem, recv_sem, peer):
        return pltpu.make_async_remote_copy(
            src_ref=src, dst_ref=dst, send_sem=send_sem, recv_sem=recv_sem, device_id=peer
        )

    def wait_bytes(like, sem):
        pltpu.make_async_copy(like, like, sem).wait()

    def rows_of(k):
        first, end = MESSAGES[k]
        return slice(16 * first, 16 * end)

    def own1(k):
        return pltpu.make_async_copy(send1.at[z, rows_of(k)], recv1.at[z, rows_of(k)], own_sem.at[k])

    def send_column(k):
        for to, peer in column:
            remote(send1.at[to, rows_of(k)], recv1.at[z, rows_of(k)], s1.at[k], r1.at[k], peer).start()
        own1(k).start()

    def store_units(kind, c, fold):
        for d in range(RING):
            for quarter in range(4):
                at = d % 4 * ROWS + quarter * UNIT
                slot = SLOT[kind, c // 2 * 4 + quarter] + c % 2 * UNIT
                send1[d, slot:slot + UNIT, :] = fold[d // 4][at:at + UNIT]

    row = lax.broadcasted_iota(jnp.int32, (LANES, LANES), 0)
    col = lax.broadcasted_iota(jnp.int32, (LANES, LANES), 1)
    diag_a, diag_v = [], []
    for c in range(COUNT):
        loads[2 + c].wait()
        mat = mats[c]
        mat32 = mat.astype(jnp.float32)
        a_up, a_low = mat32[:LANES, :LANES], mat32[LANES:, LANES:]
        store_units("a", c, [mat[:LANES, LANES:], jnp.where(row <= col, a_up, a_low).astype(jnp.bfloat16)])
        diag_a.append(jnp.sum(jnp.where(row == col, a_low, 0.0), axis=0, keepdims=True))
        if c == 1:
            pl.semaphore_wait(barrier, len(greeted))
            send_column(0)
    loads[0].wait()
    loads[1].wait()
    primal, dual = primal_ref[...], dual_ref[...]
    for c in range(COUNT):
        mat = mats[c]
        left = dot(primal, mat).astype(jnp.bfloat16)
        top = dot(left[:LANES], dual) + dot_nt(dual[:LANES], left)
        low = dot(left[LANES:], dual[:, LANES:]) + dot_nt(dual[LANES:], left[LANES:])
        corner = jnp.where(row < col, top[:, :LANES], jnp.where(row == col, 0.5 * top[:, :LANES], low))
        store_units("v", c, [top[:, LANES:].astype(jnp.bfloat16), corner.astype(jnp.bfloat16)])
        diag_v.append(jnp.sum(jnp.where(row == col, low, 0.0), axis=0, keepdims=True) * (0.5 / RING))
        if c == 1:
            for k in range(1, DIAG_MESSAGE):
                send_column(k)
    send1_diag[...] = jnp.concatenate(diag_a + diag_v, axis=0).astype(jnp.bfloat16)
    for _, peer in column:
        remote(send1_diag, recv1_diag.at[z], s1d, r1d, peer).start()
    for k in range(DIAG_MESSAGE, len(MESSAGES)):
        send_column(k)
    recv1_diag[z] = send1_diag[...]

    def block(kind, u, who):
        pair, quarter = UNITS[u]
        lanes = slice(quarter * UNIT * LANES, (quarter + 1) * UNIT * LANES)
        return v_all.at[who, pair, :, lanes] if kind == "v" else a_all.at[core, who, pair, :, lanes]

    def pass_on(u):
        wait_bytes(block("a", u, slice(0, LINE - 1)), r2a.at[u])
        whole = block("a", u, slice(None))
        remote(whole, whole, sc, rc.at[u // LAST], sibling_core).start()

    for k, (first, end) in enumerate(MESSAGES):
        own1(k).wait()
        wait_bytes(recv1.at[:RING - 1, rows_of(k)], r1.at[k])
        for kind, u in ORDER[first:end]:
            slot = SLOT[kind, u]
            for s in range(RING):
                wide_rows[slot // 16, 16 * s:16 * (s + 1), :] = recv1[s, slot:slot + 16, :].astype(jnp.float32)
            to = block(kind, u, y if kind == "v" else x)
            for r in range(UNIT):
                both = [wide_rows[slot // 16, pl.ds(half * UNIT + r, RING, stride=16), :] for half in range(2)]
                to[:, r * LANES:(r + 1) * LANES] = jnp.concatenate(both, axis=0).astype(jnp.bfloat16)
            for _, peer in (line_y if kind == "v" else line_x):
                remote(to, to, s2.at[0 if kind == "v" else 1], r2v.at[u // LAST] if kind == "v" else r2a.at[u], peer).start()
        if k == DIAG_MESSAGE:
            wait_bytes(recv1_diag.at[:RING - 1], r1d)
            for s in range(RING):
                diag_rows[pl.ds(2 * COUNT * s, 2 * COUNT), :] = recv1_diag[s].astype(jnp.float32)
            ends = [diag_rows[pl.ds(i, RING, stride=2 * COUNT), :] for i in range(2 * COUNT)]
            a_diag[core, x] = jnp.concatenate(ends[:COUNT], axis=0).astype(jnp.bfloat16)
            v_diag[y] = jnp.concatenate(ends[COUNT:], axis=0).astype(jnp.bfloat16)
            for axis, (at, line) in enumerate(((v_diag.at[y], line_y), (a_diag.at[core, x], line_x))):
                for _, peer in line:
                    remote(at, at, s2d.at[axis], r2d.at[axis], peer).start()
        if k >= 3:
            pass_on(k - 3)
    wait_bytes(a_diag.at[0, :LINE - 1], r2d.at[1])
    remote(a_diag.at[core], a_diag.at[core], s2d.at[2], r2d.at[2], sibling_core).start()
    pass_on(LAST - 1)
    pass_on(LAST)

    rows, size = LINE * COUNT * RING, 2 * LINE * COUNT * RING
    wait_bytes(v_diag.at[:LINE - 1], r2d.at[0])
    wait_bytes(a_diag.at[0], r2d.at[2])
    product = dot_nt(v_diag[...].reshape(rows, LANES), a_diag[...].reshape(size, LANES))
    most = LAST % 4 * UNIT * LANES
    seven = DEPTH * LAST // len(UNITS)
    wait_bytes(v_all.at[:LINE - 1, :, :, :seven], r2v.at[0])
    wait_bytes(a_all.at[0, :, :, :, :seven], rc.at[0])
    product += dot_nt(v_all[:, :, :, :most].reshape(rows, most), a_all[:, :, :, :, :most].reshape(size, most))
    wait_bytes(v_all.at[:LINE - 1, 0, :, most:], r2v.at[1])
    wait_bytes(a_all.at[0, :, 0, :, most:], rc.at[1])
    product += dot_nt(v_all[:, :, :, most:].reshape(rows, DEPTH - most), a_all[:, :, :, :, most:].reshape(size, DEPTH - most))
    for h in range(2):
        partial[h] = product[:, LANES * h:LANES * (h + 1)]
    own = z * LINE + y
    for z_to in range(RING):
        for h in range(2):
            piece = partial[h, pl.ds(z_to, LINE * COUNT, stride=RING), :]
            for k in range(LINE):
                send3[z_to * LINE + k, :, LANES * h:LANES * (h + 1)] = piece[COUNT * k:COUNT * (k + 1)]

    for to in [0, 8, 4, 12] + [k for k in range(32) if k not in (0, 8, 4, 12)]:
        z_to, y_to = divmod(to, LINE)

        @pl.when(own != to)
        def _():
            peer = {"wide": z_to % 4 * 16 + x * 4 + y_to, "narrow": z_to // 4 * 2 + core}
            remote(send3.at[to], recv3.at[own], s3, r3, peer).start()

    recv3[own] = send3[own]

    lane_from = lax.broadcasted_iota(jnp.int32, (size, 4 * size), 0)
    lane_to = lax.broadcasted_iota(jnp.int32, (1, 4 * size), 1)
    digit = lambda place, base=4: lax.rem(lax.div(lane_to, place), base)
    source = digit(256, 2) * 128 + digit(16) * 32 + digit(1) * 8 + digit(512, 2) * 4 + digit(64)
    source = jnp.where(digit(4) == 0, source, -1)
    pick = jnp.where(lane_from == source, 1.0, 0.0).astype(jnp.bfloat16)

    for k in range(len(MESSAGES)):
        wait_bytes(recv1.at[:RING - 1, rows_of(k)], s1.at[k])
    wait_bytes(recv1_diag.at[:RING - 1], s1d)
    wait_bytes(v_all.at[:LINE - 1], s2.at[0])
    wait_bytes(a_all.at[0, :LINE - 1], s2.at[1])
    wait_bytes(v_diag.at[:LINE - 1], s2d.at[0])
    wait_bytes(a_diag.at[0, :LINE - 1], s2d.at[1])
    wait_bytes(a_diag.at[0], s2d.at[2])
    wait_bytes(a_all.at[0], sc)
    wait_bytes(recv3.at[:RING * LINE - 1], s3)

    wait_bytes(recv3.at[:RING * LINE - 1], r3)
    totals = []
    for k in range(LINE):
        total = recv3[k]
        for z_from in range(1, RING):
            total = total + recv3[z_from * LINE + k]
        totals.append(total)
    ordered = pick_lanes(jnp.concatenate(totals, axis=0), pick)
    result = ordered[:COUNT]
    for k in range(1, LINE):
        result = result + pltpu.roll(ordered, COUNT * k, 1)[COUNT * k:COUNT * (k + 1)]
    out_ref[...] = result


def body(constraint_mats, primal_matrix, inverse_dual_iterate):
    hbm = pl.BlockSpec(memory_space=pltpu.HBM)
    dma = pltpu.SemaphoreType.DMA
    bf16, f32 = jnp.bfloat16, jnp.float32
    order = 2 * LANES
    rows, size = LINE * COUNT * RING, 2 * LINE * COUNT * RING
    return pl.pallas_call(
        kernel,
        out_shape=jax.ShapeDtypeStruct((COUNT, 1024), f32),
        in_specs=[hbm] * 3,
        out_specs=pl.BlockSpec(memory_space=pltpu.VMEM),
        scratch_shapes=[
            pltpu.VMEM((COUNT, order, order), bf16),
            pltpu.VMEM((order, order), bf16),
            pltpu.VMEM((order, order), bf16),
            pltpu.VMEM((RING, 16 * len(ORDER), LANES), bf16),
            pltpu.VMEM((RING, 16 * len(ORDER), LANES), bf16),
            pltpu.VMEM((2 * COUNT, LANES), bf16),
            pltpu.VMEM((RING, 2 * COUNT, LANES), bf16),
            pltpu.VMEM((len(ORDER), RING * 16, LANES), f32),
            pltpu.VMEM((RING * 2 * COUNT, LANES), f32),
            pltpu.VMEM((LINE, 2, 16, DEPTH), bf16),
            pltpu.VMEM((2, LINE, 2, 16, DEPTH), bf16),
            pltpu.VMEM((LINE, COUNT * RING, LANES), bf16),
            pltpu.VMEM((2, LINE, COUNT * RING, LANES), bf16),
            pltpu.VMEM((2, rows, LANES), f32),
            pltpu.VMEM((RING * LINE, COUNT, size), f32),
            pltpu.VMEM((RING * LINE, COUNT, size), f32),
            dma((COUNT + 2,)),
            dma((len(MESSAGES),)), dma((len(MESSAGES),)), dma, dma,
            dma((2,)), dma((2,)), dma((len(UNITS),)), dma((3,)), dma((3,)), dma, dma((2,)),
            dma, dma,
            dma((len(MESSAGES),)),
        ],
        compiler_params=pltpu.CompilerParams(collective_id=0, has_side_effects=True, vmem_limit_bytes=32 << 20),
        name="schur",
    )(*(pltpu.with_memory_space_constraint(m, pltpu.HBM) for m in (constraint_mats, primal_matrix, inverse_dual_iterate)))


def solution(mesh):
    in_specs = (P(("narrow", "wide"), None, None), P(), P())
    out_specs = P(("narrow", "wide"), None)
    return jax.shard_map(body, mesh=mesh, in_specs=in_specs, out_specs=out_specs, check_vma=False)
```

```python
import jax
import jax.numpy as jnp
from jax import lax
from jax.experimental import pallas as pl
from jax.experimental.pallas import tpu as pltpu
from jax.sharding import PartitionSpec as P

RING = 8
LINE = 4
COUNT = 4
LANES = 128
ROWS = 32
UNIT = 8
DEPTH = ROWS * LANES
FAR_FIRST = (4, 3, 5, 2, 6, 1, 7)
UNITS = tuple((pair, quarter) for pair in range(2) for quarter in range(4))
LAST = len(UNITS) - 1
ORDER = [("a", 0), ("a", 1), ("a", 2)] + [w for u in range(LAST - 2) for w in (("v", u), ("a", u + 3))] + [("v", LAST - 2), ("v", LAST - 1), ("v", LAST)]
SLOT = {what: 16 * i for i, what in enumerate(ORDER)}
MESSAGES = ((0, 2), (2, 4), (4, 6), (6, 8), (8, 10), (10, 12), (12, 14), (14, 15), (15, 16))
DIAG_MESSAGE = 5


def dot(a, b):
    return lax.dot_general(a, b, (((1,), (0,)), ((), ())), preferred_element_type=jnp.float32)


def dot_nt(a, b):
    return lax.dot_general(a, b, (((1,), (1,)), ((), ())), preferred_element_type=jnp.float32)


def pick_lanes(value, pick):
    high = value.astype(jnp.bfloat16)
    rest = value - high.astype(jnp.float32)
    mid = rest.astype(jnp.bfloat16)
    low = (rest - mid.astype(jnp.float32)).astype(jnp.bfloat16)
    count = value.shape[0]
    parts = dot(jnp.concatenate([high, mid, low], axis=0), pick)
    return parts[:count] + parts[count:2 * count] + parts[2 * count:]


def kernel(a_hbm, x_hbm, z_hbm, out_ref, mats, primal_ref, dual_ref, send1, recv1, send1_diag, recv1_diag, wide_rows,
           diag_rows, v_all, a_all, v_diag, a_diag, partial, send3, recv3,
           load, s1, r1, s1d, r1d, s2, r2v, r2a, s2d, r2d, sc, rc, s3, r3):
    wide, narrow = lax.axis_index("wide"), lax.axis_index("narrow")
    z_hi = lax.div(narrow, 2)
    core = narrow - 2 * z_hi
    z_lo = lax.div(wide, 16)
    plane = wide - 16 * z_lo
    x = lax.div(plane, 4)
    y = plane - 4 * x
    z = z_hi * 4 + z_lo

    def wrap(value, size):
        return jnp.where(value >= size, value - size, value)

    column = []
    for dz in FAR_FIRST:
        z_at = wrap(z + dz, RING)
        hi = jnp.where(z_at >= 4, 1, 0)
        lo = z_at - 4 * hi
        column.append((z_at, {"wide": lo * 16 + plane, "narrow": 2 * hi + core}))
    line_x, line_y = [], []
    for k in (2, 1, 3):
        x_at, y_at = wrap(x + k, LINE), wrap(y + k, LINE)
        line_x.append((x_at, {"wide": z_lo * 16 + x_at * 4 + y, "narrow": narrow}))
        line_y.append((y_at, {"wide": wide - y + y_at, "narrow": narrow}))
    sibling_core = {"wide": wide, "narrow": 2 * z_hi + 1 - core}

    barrier = pltpu.get_barrier_semaphore()
    greeted = [peer for _, peer in column + line_x + line_y] + [sibling_core]
    for peer in greeted:
        pl.semaphore_signal(barrier, inc=1, device_id=peer)

    for pair in range(2):
        pltpu.make_async_copy(a_hbm.at[2 * pair:2 * pair + 2], mats.at[2 * pair:2 * pair + 2], load.at[pair]).start()
        if pair == 0:
            pltpu.make_async_copy(x_hbm, primal_ref, load.at[2]).start()
            pltpu.make_async_copy(z_hbm, dual_ref, load.at[2]).start()

    def remote(src, dst, send_sem, recv_sem, peer):
        return pltpu.make_async_remote_copy(
            src_ref=src, dst_ref=dst, send_sem=send_sem, recv_sem=recv_sem, device_id=peer
        )

    def wait_bytes(like, sem):
        pltpu.make_async_copy(like, like, sem).wait()

    def rows_of(k):
        first, end = MESSAGES[k]
        return slice(16 * first, 16 * end)

    def own1(k):
        return pltpu.make_async_copy(send1.at[z, rows_of(k)], recv1.at[z, rows_of(k)], r1.at[k])

    def send_column(k):
        for to, peer in column:
            remote(send1.at[to, rows_of(k)], recv1.at[z, rows_of(k)], s1, r1.at[k], peer).start()
        own1(k).start()

    def store_units(kind, c, fold):
        for d in range(RING):
            for quarter in range(4):
                at = d % 4 * ROWS + quarter * UNIT
                slot = SLOT[kind, c // 2 * 4 + quarter] + c % 2 * UNIT
                send1[d, slot:slot + UNIT, :] = fold[d // 4][at:at + UNIT]

    row = lax.broadcasted_iota(jnp.int32, (LANES, LANES), 0)
    col = lax.broadcasted_iota(jnp.int32, (LANES, LANES), 1)
    diag_a, diag_v = [], []
    for c in range(COUNT):
        if c % 2 == 0:
            wait_bytes(mats.at[:2], load.at[c // 2])
        mat = mats[c]
        mat32 = mat.astype(jnp.float32)
        a_up, a_low = mat32[:LANES, :LANES], mat32[LANES:, LANES:]
        store_units("a", c, [mat[:LANES, LANES:], jnp.where(row <= col, a_up, a_low).astype(jnp.bfloat16)])
        diag_a.append(jnp.sum(jnp.where(row == col, a_low, 0.0), axis=0, keepdims=True))
        if c == 1:
            pl.semaphore_wait(barrier, len(greeted))
            send_column(0)
    wait_bytes(mats.at[:2], load.at[2])
    primal, dual = primal_ref[...], dual_ref[...]
    for c in range(COUNT):
        mat = mats[c]
        left = dot(primal, mat).astype(jnp.bfloat16)
        top = dot(left[:LANES], dual) + dot_nt(dual[:LANES], left)
        low = dot(left[LANES:], dual[:, LANES:]) + dot_nt(dual[LANES:], left[LANES:])
        corner = jnp.where(row < col, top[:, :LANES], jnp.where(row == col, 0.5 * top[:, :LANES], low))
        store_units("v", c, [top[:, LANES:].astype(jnp.bfloat16), corner.astype(jnp.bfloat16)])
        diag_v.append(jnp.sum(jnp.where(row == col, low, 0.0), axis=0, keepdims=True) * (0.5 / RING))
        if c == 1:
            for k in range(1, DIAG_MESSAGE):
                send_column(k)
    send1_diag[...] = jnp.concatenate(diag_a + diag_v, axis=0).astype(jnp.bfloat16)
    for _, peer in column:
        remote(send1_diag, recv1_diag.at[z], s1d, r1d, peer).start()
    for k in range(DIAG_MESSAGE, len(MESSAGES)):
        send_column(k)
    recv1_diag[z] = send1_diag[...]

    def block(kind, u, who):
        pair, quarter = UNITS[u]
        lanes = slice(quarter * UNIT * LANES, (quarter + 1) * UNIT * LANES)
        return v_all.at[who, pair, :, lanes] if kind == "v" else a_all.at[core, who, pair, :, lanes]

    def pass_on(u):
        wait_bytes(block("a", u, slice(0, LINE - 1)), r2a.at[u])
        whole = block("a", u, slice(None))
        remote(whole, whole, sc, rc.at[u // LAST], sibling_core).start()

    for k, (first, end) in enumerate(MESSAGES):
        wait_bytes(recv1.at[:, rows_of(k)], r1.at[k])
        for kind, u in ORDER[first:end]:
            slot = SLOT[kind, u]
            for s in range(RING):
                wide_rows[slot // 16, 16 * s:16 * (s + 1), :] = recv1[s, slot:slot + 16, :].astype(jnp.float32)
            to = block(kind, u, y if kind == "v" else x)
            for r in range(UNIT):
                both = [wide_rows[slot // 16, pl.ds(half * UNIT + r, RING, stride=16), :] for half in range(2)]
                to[:, r * LANES:(r + 1) * LANES] = jnp.concatenate(both, axis=0).astype(jnp.bfloat16)
            for _, peer in (line_y if kind == "v" else line_x):
                remote(to, to, s2, r2v.at[u // LAST] if kind == "v" else r2a.at[u], peer).start()
        if k == DIAG_MESSAGE:
            wait_bytes(recv1_diag.at[:RING - 1], r1d)
            for s in range(RING):
                diag_rows[pl.ds(2 * COUNT * s, 2 * COUNT), :] = recv1_diag[s].astype(jnp.float32)
            ends = [diag_rows[pl.ds(i, RING, stride=2 * COUNT), :] for i in range(2 * COUNT)]
            a_diag[core, x] = jnp.concatenate(ends[:COUNT], axis=0).astype(jnp.bfloat16)
            v_diag[y] = jnp.concatenate(ends[COUNT:], axis=0).astype(jnp.bfloat16)
            for axis, (at, line) in enumerate(((v_diag.at[y], line_y), (a_diag.at[core, x], line_x))):
                for _, peer in line:
                    remote(at, at, s2d.at[0], r2d.at[axis], peer).start()
        if k >= 3:
            pass_on(k - 3)
    wait_bytes(a_diag.at[0, :LINE - 1], r2d.at[1])
    remote(a_diag.at[core], a_diag.at[core], s2d.at[1], r2d.at[2], sibling_core).start()
    pass_on(LAST - 1)
    pass_on(LAST)

    rows, size = LINE * COUNT * RING, 2 * LINE * COUNT * RING
    wait_bytes(v_diag.at[:LINE - 1], r2d.at[0])
    wait_bytes(a_diag.at[0], r2d.at[2])
    product = dot_nt(v_diag[...].reshape(rows, LANES), a_diag[...].reshape(size, LANES))
    most = LAST % 4 * UNIT * LANES
    seven = DEPTH * LAST // len(UNITS)
    wait_bytes(v_all.at[:LINE - 1, :, :, :seven], r2v.at[0])
    wait_bytes(a_all.at[0, :, :, :, :seven], rc.at[0])
    product += dot_nt(v_all[:, :, :, :most].reshape(rows, most), a_all[:, :, :, :, :most].reshape(size, most))
    wait_bytes(v_all.at[:LINE - 1, 0, :, most:], r2v.at[1])
    wait_bytes(a_all.at[0, :, 0, :, most:], rc.at[1])
    product += dot_nt(v_all[:, :, :, most:].reshape(rows, DEPTH - most), a_all[:, :, :, :, most:].reshape(size, DEPTH - most))
    for h in range(2):
        partial[h] = product[:, LANES * h:LANES * (h + 1)]
    own = z * LINE + y
    for z_to in range(RING):
        for h in range(2):
            piece = partial[h, pl.ds(z_to, LINE * COUNT, stride=RING), :]
            for k in range(LINE):
                send3[z_to * LINE + k, :, LANES * h:LANES * (h + 1)] = piece[COUNT * k:COUNT * (k + 1)]

    for to in [0, 8, 4, 12] + [k for k in range(32) if k not in (0, 8, 4, 12)]:
        z_to, y_to = divmod(to, LINE)

        @pl.when(own != to)
        def _():
            peer = {"wide": z_to % 4 * 16 + x * 4 + y_to, "narrow": z_to // 4 * 2 + core}
            remote(send3.at[to], recv3.at[own], s3, r3, peer).start()

    recv3[own] = send3[own]

    lane_from = lax.broadcasted_iota(jnp.int32, (size, 4 * size), 0)
    lane_to = lax.broadcasted_iota(jnp.int32, (1, 4 * size), 1)
    digit = lambda place, base=4: lax.rem(lax.div(lane_to, place), base)
    source = digit(256, 2) * 128 + digit(16) * 32 + digit(1) * 8 + digit(512, 2) * 4 + digit(64)
    source = jnp.where(digit(4) == 0, source, -1)
    pick = jnp.where(lane_from == source, 1.0, 0.0).astype(jnp.bfloat16)

    wait_bytes(recv1.at[:RING - 1], s1)
    wait_bytes(recv1_diag.at[:RING - 1], s1d)
    wait_bytes(a_all.at[:, :LINE - 1], s2)
    wait_bytes(a_diag.at[:, :LINE - 1], s2d.at[0])
    wait_bytes(a_diag.at[0], s2d.at[1])
    wait_bytes(a_all.at[0], sc)
    wait_bytes(recv3.at[:RING * LINE - 1], s3)

    wait_bytes(recv3.at[:RING * LINE - 1], r3)
    totals = []
    for k in range(LINE):
        total = recv3[k]
        for z_from in range(1, RING):
            total = total + recv3[z_from * LINE + k]
        totals.append(total)
    ordered = pick_lanes(jnp.concatenate(totals, axis=0), pick)
    result = ordered[:COUNT]
    for k in range(1, LINE):
        result = result + pltpu.roll(ordered, COUNT * k, 1)[COUNT * k:COUNT * (k + 1)]
    out_ref[...] = result


def body(constraint_mats, primal_matrix, inverse_dual_iterate):
    hbm = pl.BlockSpec(memory_space=pltpu.HBM)
    dma = pltpu.SemaphoreType.DMA
    bf16, f32 = jnp.bfloat16, jnp.float32
    order = 2 * LANES
    rows, size = LINE * COUNT * RING, 2 * LINE * COUNT * RING
    return pl.pallas_call(
        kernel,
        out_shape=jax.ShapeDtypeStruct((COUNT, 1024), f32),
        in_specs=[hbm] * 3,
        out_specs=pl.BlockSpec(memory_space=pltpu.VMEM),
        scratch_shapes=[
            pltpu.VMEM((COUNT, order, order), bf16),
            pltpu.VMEM((order, order), bf16),
            pltpu.VMEM((order, order), bf16),
            pltpu.VMEM((RING, 16 * len(ORDER), LANES), bf16),
            pltpu.VMEM((RING, 16 * len(ORDER), LANES), bf16),
            pltpu.VMEM((2 * COUNT, LANES), bf16),
            pltpu.VMEM((RING, 2 * COUNT, LANES), bf16),
            pltpu.VMEM((len(ORDER), RING * 16, LANES), f32),
            pltpu.VMEM((RING * 2 * COUNT, LANES), f32),
            pltpu.VMEM((LINE, 2, 16, DEPTH), bf16),
            pltpu.VMEM((2, LINE, 2, 16, DEPTH), bf16),
            pltpu.VMEM((LINE, COUNT * RING, LANES), bf16),
            pltpu.VMEM((2, LINE, COUNT * RING, LANES), bf16),
            pltpu.VMEM((2, rows, LANES), f32),
            pltpu.VMEM((RING * LINE, COUNT, size), f32),
            pltpu.VMEM((RING * LINE, COUNT, size), f32),
            dma((3,)),
            dma, dma((len(MESSAGES),)), dma, dma,
            dma, dma((2,)), dma((len(UNITS),)), dma((2,)), dma((3,)), dma, dma((2,)),
            dma, dma,
        ],
        compiler_params=pltpu.CompilerParams(collective_id=0, has_side_effects=True, vmem_limit_bytes=32 << 20),
        name="schur",
    )(*(pltpu.with_memory_space_constraint(m, pltpu.HBM) for m in (constraint_mats, primal_matrix, inverse_dual_iterate)))


def solution(mesh):
    in_specs = (P(("narrow", "wide"), None, None), P(), P())
    out_specs = P(("narrow", "wide"), None)
    return jax.shard_map(body, mesh=mesh, in_specs=in_specs, out_specs=out_specs, check_vma=False)
```

```python
import jax
import jax.numpy as jnp
from jax import lax
from jax.experimental import pallas as pl
from jax.experimental.pallas import tpu as pltpu
from jax.sharding import PartitionSpec as P

RING = 8
LINE = 4
COUNT = 4
LANES = 128
ROWS = 32
UNIT = 8
DEPTH = ROWS * LANES
FAR_FIRST = (4, 3, 5, 2, 6, 1, 7)
UNITS = tuple((pair, quarter) for pair in range(2) for quarter in range(4))
LAST = len(UNITS) - 1
ORDER = [("a", 0), ("a", 1)] + [w for u in range(LAST - 1) for w in (("v", u), ("a", u + 2))] + [("v", LAST - 1), ("v", LAST)]
SLOT = {what: 16 * i for i, what in enumerate(ORDER)}
MESSAGES = ((0, 2), (2, 3), (3, 5), (5, 7), (7, 9), (9, 11), (11, 13), (13, 15), (15, 16))
DIAG_MESSAGE = 5


def dot(a, b):
    return lax.dot_general(a, b, (((1,), (0,)), ((), ())), preferred_element_type=jnp.float32)


def dot_nt(a, b):
    return lax.dot_general(a, b, (((1,), (1,)), ((), ())), preferred_element_type=jnp.float32)


def pick_lanes(value, pick):
    high = value.astype(jnp.bfloat16)
    rest = value - high.astype(jnp.float32)
    mid = rest.astype(jnp.bfloat16)
    low = (rest - mid.astype(jnp.float32)).astype(jnp.bfloat16)
    count = value.shape[0]
    parts = dot(jnp.concatenate([high, mid, low], axis=0), pick)
    return parts[:count] + parts[count:2 * count] + parts[2 * count:]


def kernel(a_hbm, x_hbm, z_hbm, out_ref, mats, primal_ref, dual_ref, send1, recv1, send1_diag, recv1_diag, wide_rows,
           diag_rows, v_all, a_all, v_diag, a_diag, partial, send3, recv3,
           load, s1, r1, s1d, r1d, s2, r2v, r2a, s2d, r2d, sc, rc, s3, r3):
    wide, narrow = lax.axis_index("wide"), lax.axis_index("narrow")
    z_hi = lax.div(narrow, 2)
    core = narrow - 2 * z_hi
    z_lo = lax.div(wide, 16)
    plane = wide - 16 * z_lo
    x = lax.div(plane, 4)
    y = plane - 4 * x
    z = z_hi * 4 + z_lo

    def wrap(value, size):
        return jnp.where(value >= size, value - size, value)

    column = []
    for dz in FAR_FIRST:
        z_at = wrap(z + dz, RING)
        hi = jnp.where(z_at >= 4, 1, 0)
        lo = z_at - 4 * hi
        column.append((z_at, {"wide": lo * 16 + plane, "narrow": 2 * hi + core}))
    line_x, line_y = [], []
    for k in (2, 1, 3):
        x_at, y_at = wrap(x + k, LINE), wrap(y + k, LINE)
        line_x.append((x_at, {"wide": z_lo * 16 + x_at * 4 + y, "narrow": narrow}))
        line_y.append((y_at, {"wide": wide - y + y_at, "narrow": narrow}))
    sibling_core = {"wide": wide, "narrow": 2 * z_hi + 1 - core}

    barrier = pltpu.get_barrier_semaphore()
    greeted = [peer for _, peer in column + line_x + line_y] + [sibling_core]
    for peer in greeted:
        pl.semaphore_signal(barrier, inc=1, device_id=peer)

    for pair in range(2):
        pltpu.make_async_copy(a_hbm.at[2 * pair:2 * pair + 2], mats.at[2 * pair:2 * pair + 2], load.at[pair]).start()
        if pair == 0:
            pltpu.make_async_copy(x_hbm, primal_ref, load.at[2]).start()
            pltpu.make_async_copy(z_hbm, dual_ref, load.at[2]).start()

    def remote(src, dst, send_sem, recv_sem, peer):
        return pltpu.make_async_remote_copy(
            src_ref=src, dst_ref=dst, send_sem=send_sem, recv_sem=recv_sem, device_id=peer
        )

    def wait_bytes(like, sem):
        pltpu.make_async_copy(like, like, sem).wait()

    def rows_of(k):
        first, end = MESSAGES[k]
        return slice(16 * first, 16 * end)

    def own1(k):
        return pltpu.make_async_copy(send1.at[z, rows_of(k)], recv1.at[z, rows_of(k)], r1.at[k])

    def send_column(k):
        for to, peer in column:
            remote(send1.at[to, rows_of(k)], recv1.at[z, rows_of(k)], s1, r1.at[k], peer).start()
        own1(k).start()

    def store_units(kind, c, fold):
        for d in range(RING):
            for quarter in range(4):
                at = d % 4 * ROWS + quarter * UNIT
                slot = SLOT[kind, c // 2 * 4 + quarter] + c % 2 * UNIT
                send1[d, slot:slot + UNIT, :] = fold[d // 4][at:at + UNIT]

    row = lax.broadcasted_iota(jnp.int32, (LANES, LANES), 0)
    col = lax.broadcasted_iota(jnp.int32, (LANES, LANES), 1)
    diag_a, diag_v = [], []
    for c in range(COUNT):
        if c % 2 == 0:
            wait_bytes(mats.at[:2], load.at[c // 2])
        mat = mats[c]
        mat32 = mat.astype(jnp.float32)
        a_up, a_low = mat32[:LANES, :LANES], mat32[LANES:, LANES:]
        store_units("a", c, [mat[:LANES, LANES:], jnp.where(row <= col, a_up, a_low).astype(jnp.bfloat16)])
        diag_a.append(jnp.sum(jnp.where(row == col, a_low, 0.0), axis=0, keepdims=True))
        if c == 1:
            pl.semaphore_wait(barrier, len(greeted))
            send_column(0)
    wait_bytes(mats.at[:2], load.at[2])
    primal, dual = primal_ref[...], dual_ref[...]
    for c in range(COUNT):
        mat = mats[c]
        left = dot(primal, mat).astype(jnp.bfloat16)
        top = dot(left[:LANES], dual) + dot_nt(dual[:LANES], left)
        low = dot(left[LANES:], dual[:, LANES:]) + dot_nt(dual[LANES:], left[LANES:])
        corner = jnp.where(row < col, top[:, :LANES], jnp.where(row == col, 0.5 * top[:, :LANES], low))
        store_units("v", c, [top[:, LANES:].astype(jnp.bfloat16), corner.astype(jnp.bfloat16)])
        diag_v.append(jnp.sum(jnp.where(row == col, low, 0.0), axis=0, keepdims=True) * (0.5 / RING))
        if c == 1:
            for k in range(1, DIAG_MESSAGE):
                send_column(k)
    send1_diag[...] = jnp.concatenate(diag_a + diag_v, axis=0).astype(jnp.bfloat16)
    for _, peer in column:
        remote(send1_diag, recv1_diag.at[z], s1d, r1d, peer).start()
    for k in range(DIAG_MESSAGE, len(MESSAGES)):
        send_column(k)
    recv1_diag[z] = send1_diag[...]

    def block(kind, u, who):
        pair, quarter = UNITS[u]
        lanes = slice(quarter * UNIT * LANES, (quarter + 1) * UNIT * LANES)
        return v_all.at[who, pair, :, lanes] if kind == "v" else a_all.at[core, who, pair, :, lanes]

    def pass_on(u):
        wait_bytes(block("a", u, slice(0, LINE - 1)), r2a.at[u])
        whole = block("a", u, slice(None))
        remote(whole, whole, sc, rc.at[u // LAST], sibling_core).start()

    for k, (first, end) in enumerate(MESSAGES):
        wait_bytes(recv1.at[:, rows_of(k)], r1.at[k])
        for kind, u in ORDER[first:end]:
            slot = SLOT[kind, u]
            for s in range(RING):
                wide_rows[slot // 16, 16 * s:16 * (s + 1), :] = recv1[s, slot:slot + 16, :].astype(jnp.float32)
            to = block(kind, u, y if kind == "v" else x)
            for r in range(UNIT):
                both = [wide_rows[slot // 16, pl.ds(half * UNIT + r, RING, stride=16), :] for half in range(2)]
                to[:, r * LANES:(r + 1) * LANES] = jnp.concatenate(both, axis=0).astype(jnp.bfloat16)
            for _, peer in (line_y if kind == "v" else line_x):
                remote(to, to, s2, r2v.at[u // LAST] if kind == "v" else r2a.at[u], peer).start()
        if k == DIAG_MESSAGE:
            wait_bytes(recv1_diag.at[:RING - 1], r1d)
            for s in range(RING):
                diag_rows[pl.ds(2 * COUNT * s, 2 * COUNT), :] = recv1_diag[s].astype(jnp.float32)
            ends = [diag_rows[pl.ds(i, RING, stride=2 * COUNT), :] for i in range(2 * COUNT)]
            a_diag[core, x] = jnp.concatenate(ends[:COUNT], axis=0).astype(jnp.bfloat16)
            v_diag[y] = jnp.concatenate(ends[COUNT:], axis=0).astype(jnp.bfloat16)
            for axis, (at, line) in enumerate(((v_diag.at[y], line_y), (a_diag.at[core, x], line_x))):
                for _, peer in line:
                    remote(at, at, s2d.at[0], r2d.at[axis], peer).start()
        if k >= 4:
            pass_on(k - 4)
    wait_bytes(a_diag.at[0, :LINE - 1], r2d.at[1])
    remote(a_diag.at[core], a_diag.at[core], s2d.at[1], r2d.at[2], sibling_core).start()
    for u in range(LAST - 2, LAST + 1):
        pass_on(u)

    rows, size = LINE * COUNT * RING, 2 * LINE * COUNT * RING
    wait_bytes(v_diag.at[:LINE - 1], r2d.at[0])
    wait_bytes(a_diag.at[0], r2d.at[2])
    product = dot_nt(v_diag[...].reshape(rows, LANES), a_diag[...].reshape(size, LANES))
    most = LAST % 4 * UNIT * LANES
    seven = DEPTH * LAST // len(UNITS)
    wait_bytes(v_all.at[:LINE - 1, :, :, :seven], r2v.at[0])
    wait_bytes(a_all.at[0, :, :, :, :seven], rc.at[0])
    product += dot_nt(v_all[:, :, :, :most].reshape(rows, most), a_all[:, :, :, :, :most].reshape(size, most))
    wait_bytes(v_all.at[:LINE - 1, 0, :, most:], r2v.at[1])
    wait_bytes(a_all.at[0, :, 0, :, most:], rc.at[1])
    product += dot_nt(v_all[:, :, :, most:].reshape(rows, DEPTH - most), a_all[:, :, :, :, most:].reshape(size, DEPTH - most))
    for h in range(2):
        partial[h] = product[:, LANES * h:LANES * (h + 1)]
    own = z * LINE + y
    for z_to in range(RING):
        for h in range(2):
            piece = partial[h, pl.ds(z_to, LINE * COUNT, stride=RING), :]
            for k in range(LINE):
                send3[z_to * LINE + k, :, LANES * h:LANES * (h + 1)] = piece[COUNT * k:COUNT * (k + 1)]

    for to in [0, 8, 4, 12] + [k for k in range(32) if k not in (0, 8, 4, 12)]:
        z_to, y_to = divmod(to, LINE)

        @pl.when(own != to)
        def _():
            peer = {"wide": z_to % 4 * 16 + x * 4 + y_to, "narrow": z_to // 4 * 2 + core}
            remote(send3.at[to], recv3.at[own], s3, r3, peer).start()

    recv3[own] = send3[own]

    lane_from = lax.broadcasted_iota(jnp.int32, (size, 4 * size), 0)
    lane_to = lax.broadcasted_iota(jnp.int32, (1, 4 * size), 1)
    digit = lambda place, base=4: lax.rem(lax.div(lane_to, place), base)
    source = digit(256, 2) * 128 + digit(16) * 32 + digit(1) * 8 + digit(512, 2) * 4 + digit(64)
    source = jnp.where(digit(4) == 0, source, -1)
    pick = jnp.where(lane_from == source, 1.0, 0.0).astype(jnp.bfloat16)

    wait_bytes(recv1.at[:RING - 1], s1)
    wait_bytes(recv1_diag.at[:RING - 1], s1d)
    wait_bytes(a_all.at[:, :LINE - 1], s2)
    wait_bytes(a_diag.at[:, :LINE - 1], s2d.at[0])
    wait_bytes(a_diag.at[0], s2d.at[1])
    wait_bytes(a_all.at[0], sc)
    wait_bytes(recv3.at[:RING * LINE - 1], s3)

    wait_bytes(recv3.at[:RING * LINE - 1], r3)
    totals = []
    for k in range(LINE):
        total = recv3[k]
        for z_from in range(1, RING):
            total = total + recv3[z_from * LINE + k]
        totals.append(total)
    ordered = pick_lanes(jnp.concatenate(totals, axis=0), pick)
    result = ordered[:COUNT]
    for k in range(1, LINE):
        result = result + pltpu.roll(ordered[COUNT * k:COUNT * (k + 1)], COUNT * k, 1)
    out_ref[...] = result


def body(constraint_mats, primal_matrix, inverse_dual_iterate):
    hbm = pl.BlockSpec(memory_space=pltpu.HBM)
    dma = pltpu.SemaphoreType.DMA
    bf16, f32 = jnp.bfloat16, jnp.float32
    order = 2 * LANES
    rows, size = LINE * COUNT * RING, 2 * LINE * COUNT * RING
    return pl.pallas_call(
        kernel,
        out_shape=jax.ShapeDtypeStruct((COUNT, 1024), f32),
        in_specs=[hbm] * 3,
        out_specs=pl.BlockSpec(memory_space=pltpu.VMEM),
        scratch_shapes=[
            pltpu.VMEM((COUNT, order, order), bf16),
            pltpu.VMEM((order, order), bf16),
            pltpu.VMEM((order, order), bf16),
            pltpu.VMEM((RING, 16 * len(ORDER), LANES), bf16),
            pltpu.VMEM((RING, 16 * len(ORDER), LANES), bf16),
            pltpu.VMEM((2 * COUNT, LANES), bf16),
            pltpu.VMEM((RING, 2 * COUNT, LANES), bf16),
            pltpu.VMEM((len(ORDER), RING * 16, LANES), f32),
            pltpu.VMEM((RING * 2 * COUNT, LANES), f32),
            pltpu.VMEM((LINE, 2, 16, DEPTH), bf16),
            pltpu.VMEM((2, LINE, 2, 16, DEPTH), bf16),
            pltpu.VMEM((LINE, COUNT * RING, LANES), bf16),
            pltpu.VMEM((2, LINE, COUNT * RING, LANES), bf16),
            pltpu.VMEM((2, rows, LANES), f32),
            pltpu.VMEM((RING * LINE, COUNT, size), f32),
            pltpu.VMEM((RING * LINE, COUNT, size), f32),
            dma((3,)),
            dma, dma((len(MESSAGES),)), dma, dma,
            dma, dma((2,)), dma((len(UNITS),)), dma((2,)), dma((3,)), dma, dma((2,)),
            dma, dma,
        ],
        compiler_params=pltpu.CompilerParams(collective_id=0, has_side_effects=True, vmem_limit_bytes=32 << 20),
        name="schur",
    )(*(pltpu.with_memory_space_constraint(m, pltpu.HBM) for m in (constraint_mats, primal_matrix, inverse_dual_iterate)))


def solution(mesh):
    in_specs = (P(("narrow", "wide"), None, None), P(), P())
    out_specs = P(("narrow", "wide"), None)
    return jax.shard_map(body, mesh=mesh, in_specs=in_specs, out_specs=out_specs, check_vma=False)
```

```python
import jax
import jax.numpy as jnp
from jax import lax
from jax.experimental import pallas as pl
from jax.experimental.pallas import tpu as pltpu
from jax.sharding import PartitionSpec as P

RING = 8
LINE = 4
COUNT = 4
LANES = 128
ROWS = 32
UNIT = 8
DEPTH = ROWS * LANES
FAR_FIRST = (4, 3, 5, 2, 6, 1, 7)
UNITS = tuple((pair, quarter) for pair in range(2) for quarter in range(4))
LAST = len(UNITS) - 1
ORDER = [("a", 0), ("a", 1), ("a", 2)] + [w for u in range(LAST - 2) for w in (("v", u), ("a", u + 3))] + [("v", LAST - 2), ("v", LAST - 1), ("v", LAST)]
SLOT = {what: 16 * i for i, what in enumerate(ORDER)}
MESSAGES = ((0, 2), (2, 4), (4, 6), (6, 8), (8, 10), (10, 12), (12, 14), (14, 15), (15, 16))
DIAG_MESSAGE = 5


def dot(a, b):
    return lax.dot_general(a, b, (((1,), (0,)), ((), ())), preferred_element_type=jnp.float32)


def dot_nt(a, b):
    return lax.dot_general(a, b, (((1,), (1,)), ((), ())), preferred_element_type=jnp.float32)


def pick_lanes(value, pick):
    high = value.astype(jnp.bfloat16)
    rest = value - high.astype(jnp.float32)
    mid = rest.astype(jnp.bfloat16)
    low = (rest - mid.astype(jnp.float32)).astype(jnp.bfloat16)
    count = value.shape[0]
    parts = dot(jnp.concatenate([high, mid, low], axis=0), pick)
    return parts[:count] + parts[count:2 * count] + parts[2 * count:]


def kernel(a_hbm, x_hbm, z_hbm, out_ref, mats, primal_ref, dual_ref, send1, recv1, send1_diag, recv1_diag, wide_rows,
           diag_rows, v_all, a_all, v_diag, a_diag, partial, send3, recv3,
           load, s1, r1, s1d, r1d, s2, r2v, r2a, s2d, r2d, sc, rc, s3, r3):
    wide, narrow = lax.axis_index("wide"), lax.axis_index("narrow")
    z_hi = lax.div(narrow, 2)
    core = narrow - 2 * z_hi
    z_lo = lax.div(wide, 16)
    plane = wide - 16 * z_lo
    x = lax.div(plane, 4)
    y = plane - 4 * x
    z = z_hi * 4 + z_lo

    def wrap(value, size):
        return jnp.where(value >= size, value - size, value)

    column = []
    for dz in FAR_FIRST:
        z_at = wrap(z + dz, RING)
        hi = jnp.where(z_at >= 4, 1, 0)
        lo = z_at - 4 * hi
        column.append((z_at, {"wide": lo * 16 + plane, "narrow": 2 * hi + core}))
    line_x, line_y = [], []
    for k in (2, 1, 3):
        x_at, y_at = wrap(x + k, LINE), wrap(y + k, LINE)
        line_x.append((x_at, {"wide": z_lo * 16 + x_at * 4 + y, "narrow": narrow}))
        line_y.append((y_at, {"wide": wide - y + y_at, "narrow": narrow}))
    sibling_core = {"wide": wide, "narrow": 2 * z_hi + 1 - core}

    barrier = pltpu.get_barrier_semaphore()
    greeted = [peer for _, peer in column + line_x + line_y] + [sibling_core]
    for peer in greeted:
        pl.semaphore_signal(barrier, inc=1, device_id=peer)

    for pair in range(2):
        pltpu.make_async_copy(a_hbm.at[2 * pair:2 * pair + 2], mats.at[2 * pair:2 * pair + 2], load.at[pair]).start()
        if pair == 0:
            pltpu.make_async_copy(x_hbm, primal_ref, load.at[2]).start()
            pltpu.make_async_copy(z_hbm, dual_ref, load.at[2]).start()

    def remote(src, dst, send_sem, recv_sem, peer):
        return pltpu.make_async_remote_copy(
            src_ref=src, dst_ref=dst, send_sem=send_sem, recv_sem=recv_sem, device_id=peer
        )

    def wait_bytes(like, sem):
        pltpu.make_async_copy(like, like, sem).wait()

    def rows_of(k):
        first, end = MESSAGES[k]
        return slice(16 * first, 16 * end)

    def own1(k):
        return pltpu.make_async_copy(send1.at[z, rows_of(k)], recv1.at[z, rows_of(k)], r1.at[k])

    def send_column(k):
        for to, peer in column:
            remote(send1.at[to, rows_of(k)], recv1.at[z, rows_of(k)], s1, r1.at[k], peer).start()
        own1(k).start()

    def store_units(kind, c, fold):
        for d in range(RING):
            for quarter in range(4):
                at = d % 4 * ROWS + quarter * UNIT
                slot = SLOT[kind, c // 2 * 4 + quarter] + c % 2 * UNIT
                send1[d, slot:slot + UNIT, :] = fold[d // 4][at:at + UNIT]

    row = lax.broadcasted_iota(jnp.int32, (LANES, LANES), 0)
    col = lax.broadcasted_iota(jnp.int32, (LANES, LANES), 1)
    diag_a, diag_v = [], []
    for c in range(COUNT):
        if c % 2 == 0:
            wait_bytes(mats.at[:2], load.at[c // 2])
        mat = mats[c]
        mat32 = mat.astype(jnp.float32)
        a_up, a_low = mat32[:LANES, :LANES], mat32[LANES:, LANES:]
        store_units("a", c, [mat[:LANES, LANES:], jnp.where(row <= col, a_up, a_low).astype(jnp.bfloat16)])
        diag_a.append(jnp.sum(jnp.where(row == col, a_low, 0.0), axis=0, keepdims=True))
        if c == 1:
            pl.semaphore_wait(barrier, len(greeted))
            send_column(0)
    wait_bytes(mats.at[:2], load.at[2])
    primal, dual = primal_ref[...], dual_ref[...]
    for c in range(COUNT):
        mat = mats[c]
        left = dot(primal, mat).astype(jnp.bfloat16)
        top = dot(left[:LANES], dual) + dot_nt(dual[:LANES], left)
        low = dot(left[LANES:], dual[:, LANES:]) + dot_nt(dual[LANES:], left[LANES:])
        corner = jnp.where(row < col, top[:, :LANES], jnp.where(row == col, 0.5 * top[:, :LANES], low))
        store_units("v", c, [top[:, LANES:].astype(jnp.bfloat16), corner.astype(jnp.bfloat16)])
        diag_v.append(jnp.sum(jnp.where(row == col, low, 0.0), axis=0, keepdims=True) * (0.5 / RING))
        if c == 1:
            for k in range(1, DIAG_MESSAGE):
                send_column(k)
    send1_diag[...] = jnp.concatenate(diag_a + diag_v, axis=0).astype(jnp.bfloat16)
    for _, peer in column:
        remote(send1_diag, recv1_diag.at[z], s1d, r1d, peer).start()
    for k in range(DIAG_MESSAGE, len(MESSAGES)):
        send_column(k)
    recv1_diag[z] = send1_diag[...]

    def block(kind, u, who):
        pair, quarter = UNITS[u]
        lanes = slice(quarter * UNIT * LANES, (quarter + 1) * UNIT * LANES)
        return v_all.at[who, pair, :, lanes] if kind == "v" else a_all.at[core, who, pair, :, lanes]

    def pass_on(u):
        wait_bytes(block("a", u, slice(0, LINE - 1)), r2a.at[u])
        whole = block("a", u, slice(None))
        remote(whole, whole, sc, rc.at[u // LAST], sibling_core).start()

    for k, (first, end) in enumerate(MESSAGES):
        wait_bytes(recv1.at[:, rows_of(k)], r1.at[k])
        for kind, u in ORDER[first:end]:
            slot = SLOT[kind, u]
            for s in range(RING):
                wide_rows[slot // 16, 16 * s:16 * (s + 1), :] = recv1[s, slot:slot + 16, :].astype(jnp.float32)
            to = block(kind, u, y if kind == "v" else x)
            for r in range(UNIT):
                both = [wide_rows[slot // 16, pl.ds(half * UNIT + r, RING, stride=16), :] for half in range(2)]
                to[:, r * LANES:(r + 1) * LANES] = jnp.concatenate(both, axis=0).astype(jnp.bfloat16)
            for _, peer in (line_y if kind == "v" else line_x):
                remote(to, to, s2, r2v.at[u // LAST] if kind == "v" else r2a.at[u], peer).start()
        if k == DIAG_MESSAGE:
            wait_bytes(recv1_diag.at[:RING - 1], r1d)
            for s in range(RING):
                diag_rows[pl.ds(2 * COUNT * s, 2 * COUNT), :] = recv1_diag[s].astype(jnp.float32)
            ends = [diag_rows[pl.ds(i, RING, stride=2 * COUNT), :] for i in range(2 * COUNT)]
            a_diag[core, x] = jnp.concatenate(ends[:COUNT], axis=0).astype(jnp.bfloat16)
            v_diag[y] = jnp.concatenate(ends[COUNT:], axis=0).astype(jnp.bfloat16)
            for axis, (at, line) in enumerate(((v_diag.at[y], line_y), (a_diag.at[core, x], line_x))):
                for _, peer in line:
                    remote(at, at, s2d.at[0], r2d.at[axis], peer).start()
        if k >= 3:
            pass_on(k - 3)
    wait_bytes(a_diag.at[0, :LINE - 1], r2d.at[1])
    remote(a_diag.at[core], a_diag.at[core], s2d.at[1], r2d.at[2], sibling_core).start()
    pass_on(LAST - 1)
    pass_on(LAST)

    rows, size = LINE * COUNT * RING, 2 * LINE * COUNT * RING
    wait_bytes(v_diag.at[:LINE - 1], r2d.at[0])
    wait_bytes(a_diag.at[0], r2d.at[2])
    product = dot_nt(v_diag[...].reshape(rows, LANES), a_diag[...].reshape(size, LANES))
    most = LAST % 4 * UNIT * LANES
    seven = DEPTH * LAST // len(UNITS)
    wait_bytes(v_all.at[:LINE - 1, :, :, :seven], r2v.at[0])
    wait_bytes(a_all.at[0, :, :, :, :seven], rc.at[0])
    product += dot_nt(v_all[:, :, :, :most].reshape(rows, most), a_all[:, :, :, :, :most].reshape(size, most))
    wait_bytes(v_all.at[:LINE - 1, 0, :, most:], r2v.at[1])
    wait_bytes(a_all.at[0, :, 0, :, most:], rc.at[1])
    product += dot_nt(v_all[:, :, :, most:].reshape(rows, DEPTH - most), a_all[:, :, :, :, most:].reshape(size, DEPTH - most))
    for h in range(2):
        partial[h] = product[:, LANES * h:LANES * (h + 1)]
    own = z * LINE + y
    for z_to in range(RING):
        for h in range(2):
            piece = partial[h, pl.ds(z_to, LINE * COUNT, stride=RING), :]
            for k in range(LINE):
                send3[z_to * LINE + k, :, LANES * h:LANES * (h + 1)] = piece[COUNT * k:COUNT * (k + 1)]

    for to in [0, 8, 4, 12] + [k for k in range(32) if k not in (0, 8, 4, 12)]:
        z_to, y_to = divmod(to, LINE)

        @pl.when(own != to)
        def _():
            peer = {"wide": z_to % 4 * 16 + x * 4 + y_to, "narrow": z_to // 4 * 2 + core}
            remote(send3.at[to], recv3.at[own], s3, r3, peer).start()

    recv3[own] = send3[own]

    lane_from = lax.broadcasted_iota(jnp.int32, (size, 4 * size), 0)
    lane_to = lax.broadcasted_iota(jnp.int32, (1, 4 * size), 1)
    digit = lambda place, base=4: lax.rem(lax.div(lane_to, place), base)
    source = digit(256, 2) * 128 + digit(16) * 32 + digit(1) * 8 + digit(512, 2) * 4 + digit(64)
    source = jnp.where(digit(4) == 0, source, -1)
    pick = jnp.where(lane_from == source, 1.0, 0.0).astype(jnp.bfloat16)

    wait_bytes(recv1.at[:RING - 1], s1)
    wait_bytes(recv1_diag.at[:RING - 1], s1d)
    wait_bytes(a_all.at[:, :LINE - 1], s2)
    wait_bytes(a_diag.at[:, :LINE - 1], s2d.at[0])
    wait_bytes(a_diag.at[0], s2d.at[1])
    wait_bytes(a_all.at[0], sc)
    wait_bytes(recv3.at[:RING * LINE - 1], s3)

    wait_bytes(recv3.at[:RING * LINE - 1], r3)
    totals = []
    for k in range(LINE):
        total = recv3[k]
        for z_from in range(1, RING):
            total = total + recv3[z_from * LINE + k]
        totals.append(total)
    ordered = pick_lanes(jnp.concatenate(totals, axis=0), pick)
    result = ordered[:COUNT]
    for k in range(1, LINE):
        result = result + pltpu.roll(ordered[COUNT * k:COUNT * (k + 1)], COUNT * k, 1)
    out_ref[...] = result


def body(constraint_mats, primal_matrix, inverse_dual_iterate):
    hbm = pl.BlockSpec(memory_space=pltpu.HBM)
    dma = pltpu.SemaphoreType.DMA
    bf16, f32 = jnp.bfloat16, jnp.float32
    order = 2 * LANES
    rows, size = LINE * COUNT * RING, 2 * LINE * COUNT * RING
    return pl.pallas_call(
        kernel,
        out_shape=jax.ShapeDtypeStruct((COUNT, 1024), f32),
        in_specs=[hbm] * 3,
        out_specs=pl.BlockSpec(memory_space=pltpu.VMEM),
        scratch_shapes=[
            pltpu.VMEM((COUNT, order, order), bf16),
            pltpu.VMEM((order, order), bf16),
            pltpu.VMEM((order, order), bf16),
            pltpu.VMEM((RING, 16 * len(ORDER), LANES), bf16),
            pltpu.VMEM((RING, 16 * len(ORDER), LANES), bf16),
            pltpu.VMEM((2 * COUNT, LANES), bf16),
            pltpu.VMEM((RING, 2 * COUNT, LANES), bf16),
            pltpu.VMEM((len(ORDER), RING * 16, LANES), f32),
            pltpu.VMEM((RING * 2 * COUNT, LANES), f32),
            pltpu.VMEM((LINE, 2, 16, DEPTH), bf16),
            pltpu.VMEM((2, LINE, 2, 16, DEPTH), bf16),
            pltpu.VMEM((LINE, COUNT * RING, LANES), bf16),
            pltpu.VMEM((2, LINE, COUNT * RING, LANES), bf16),
            pltpu.VMEM((2, rows, LANES), f32),
            pltpu.VMEM((RING * LINE, COUNT, size), f32),
            pltpu.VMEM((RING * LINE, COUNT, size), f32),
            dma((3,)),
            dma, dma((len(MESSAGES),)), dma, dma,
            dma, dma((2,)), dma((len(UNITS),)), dma((2,)), dma((3,)), dma, dma((2,)),
            dma, dma,
        ],
        compiler_params=pltpu.CompilerParams(collective_id=0, has_side_effects=True, vmem_limit_bytes=32 << 20),
        name="schur",
    )(*(pltpu.with_memory_space_constraint(m, pltpu.HBM) for m in (constraint_mats, primal_matrix, inverse_dual_iterate)))


def solution(mesh):
    in_specs = (P(("narrow", "wide"), None, None), P(), P())
    out_specs = P(("narrow", "wide"), None)
    return jax.shard_map(body, mesh=mesh, in_specs=in_specs, out_specs=out_specs, check_vma=False)
```
